512 devices in a mesh: gy: 16 (over y, core), gz: 32 (over x, z).
Axes of the slice: x: 4, y: 8, z: 8, core: 2. Of those that a mesh axis runs over, the one named last changes fastest.
Arguments:
- fields: float32 [3, 132, 256, 4096], P(None, None, 'gy', 'gz'), may hold values from -25 to 25
Outputs:
- enstrophy: float32 [128, 256, 4096], P(None, 'gy', 'gz')
- strain_rate: float32 [128, 256, 4096], P(None, 'gy', 'gz')
- factor: float32 [128, 128], replicated
The draws below stay inside these ranges and needn't reach their ends.
All inputs are finite; a program needn't handle non-finite values.
Results may differ from the reference program's by a relative error of at most 0.0003.
Values sent between devices are 32-bit elements; how exact they have to be, the bound alone decides.
A program may use at most 64 MiB of HBM per device.

```python
import jax
import jax.numpy as jnp
from jax import lax

X = 128
NY = 256
NZ = 4096


def draw_fields(key, part):
    key_base = jax.random.fold_in(key, 11)
    key_rough = jax.random.fold_in(key, 12)
    array_shape = (3, X + 4, NY, NZ)
    baseline = jax.random.truncated_normal(key_base, -4.0, 4.0, array_shape, jnp.float32)
    roughness = jnp.exp(jax.random.uniform(key_rough, array_shape, jnp.float32, -0.7, 0.7))
    y_position = jnp.arange(NY, dtype=jnp.float32) / max(NY - 1, 1)
    z_position = jnp.arange(NZ, dtype=jnp.float32) / max(NZ - 1, 1)
    envelope = jnp.sqrt((1.0 + 2.0 * y_position)[:, None] * (1.0 + 2.0 * z_position)[None, :])
    values = baseline * roughness * envelope
    return values


def setup_inputs(seed: int = 0) -> dict:
    seeds = jax.random.split(jax.random.key(seed), 2)
    return {
        "fields": draw_fields(jax.random.fold_in(seeds[1], 71), 0),
    }


def stencil(minus_two, minus_one, plus_one, plus_two):
    return (minus_two - 8.0 * minus_one + 8.0 * plus_one - plus_two) / 12.0

def periodic(values, axis_number):
    return stencil(jnp.roll(values, 2, axis_number), jnp.roll(values, 1, axis_number), jnp.roll(values, -1, axis_number), jnp.roll(values, -2, axis_number))

def invariants(along_x, along_y, along_z):
    gradient = (along_x, along_y, along_z)
    strain_rate = gradient[0][0] * gradient[0][0] + gradient[1][1] * gradient[1][1] + gradient[2][2] * gradient[2][2]
    enstrophy = jnp.zeros_like(strain_rate)
    for source_axis, target_axis in ((0, 1), (0, 2), (1, 2)):
        rotation = gradient[source_axis][target_axis] - gradient[target_axis][source_axis]
        shearing = gradient[source_axis][target_axis] + gradient[target_axis][source_axis]
        enstrophy = enstrophy + 0.5 * rotation * rotation
        strain_rate = strain_rate + 0.5 * shearing * shearing
    return (enstrophy, strain_rate)

def reference(fields):
    per_block = 8

    def one_block(block_index):
        first_plane = (block_index * per_block).astype(jnp.int32)
        slab_planes = lax.dynamic_slice_in_dim(fields, first_plane, per_block + 4, 1)
        centre = slab_planes[:, 2:per_block + 2]
        along_x = stencil(slab_planes[:, 0:per_block], slab_planes[:, 1:per_block + 1], slab_planes[:, 3:per_block + 3], slab_planes[:, 4:per_block + 4])
        along_y = periodic(centre, 2)
        along_z = periodic(centre, 3)
        return invariants(along_x, along_y, along_z)
    enstrophy, strain_rate = lax.map(one_block, jnp.arange(X // per_block, dtype=jnp.int32))
    enstrophy = enstrophy.reshape(X, NY, NZ)
    strain_rate = strain_rate.reshape(X, NY, NZ)
    cell_count = NY * NZ
    matrices = (fields[0, 2:X + 2].reshape(X, cell_count), fields[1, 2:X + 2].reshape(X, cell_count), fields[2, 2:X + 2].reshape(X, cell_count), enstrophy.reshape(X, cell_count), strain_rate.reshape(X, cell_count))
    cross = jnp.zeros((X, X), jnp.float32)
    for matrix in matrices:
        gram = jnp.dot(matrix.astype(jnp.float32), matrix.T.astype(jnp.float32), precision=lax.Precision.HIGHEST, preferred_element_type=jnp.float32)
        mean_square = jnp.sum(matrix * matrix) / (X * cell_count)
        cross = cross + gram / (5.0 * cell_count * (mean_square + 1e-06))
    factor = jnp.linalg.cholesky(cross)
    return (enstrophy, strain_rate, factor)
```

```python
import jax
import jax.numpy as jnp
from jax import lax
from jax.experimental import pallas as pl
from jax.experimental.pallas import tpu as pltpu
from jax.sharding import PartitionSpec as P

MESH = pl.DeviceIdType.MESH
CORES = 2
N = 128
RY = 16
RZ = 128
X0 = 6
XC = X0 + 2
XB = 16
F32 = jnp.float32
BF16 = jnp.bfloat16


def ring_order(count):
    return sorted(range(1, count), key=lambda k: -min(k, count - k))


def main_kernel(
    sizes,
    fields,
    enst,
    strn,
    cross_out,
    fld,
    pack_r,
    pack_l,
    from_left,
    from_right,
    merged,
    dxw_buf,
    dyw_buf,
    halves,
    piece,
    recv_a,
    sum_a,
    recv_b,
    sum_b,
    recv_c,
    comb,
    load_sem,
    halo_send,
    halo_recv,
    rs_send,
    rs_recv,
    ey_send,
    ey_recv,
    ez_send,
    ez_recv,
    ag_send,
    ag_recv,
):
    gy, gz, zc = sizes
    yc, xc = gy // CORES, gz // zc
    owners = xc * CORES
    own_rows = N // owners
    cells = gy * RY * gz * RZ
    g, h = lax.axis_index("gy"), lax.axis_index("gz")
    y, c = g // CORES, g % CORES
    x, z = h // zc, h % zc

    rs_peers = []
    for dx in ring_order(xc) + [0]:
        for dc in range(CORES):
            if dx or dc:
                slot = dx * CORES + dc - 1
                px, pc = lax.rem(x + dx, xc), lax.rem(c + dc, CORES)
                rs_peers.append((slot, px * CORES + pc, (y * CORES + pc, px * zc + z)))
    ey_peers = [(k - 1, (lax.rem(y + k, yc) * CORES + c, h)) for k in ring_order(yc)]
    ez_peers = [(k - 1, (g, x * zc + lax.rem(z + k, zc))) for k in ring_order(zc)]
    me = x * CORES + c
    up, down = (lax.rem(g + 1, gy), h), (lax.rem(g + gy - 1, gy), h)
    right, left = (g, lax.rem(h + 1, gz)), (g, lax.rem(h + gz - 1, gz))

    barrier = pltpu.get_barrier_semaphore()
    peers = [p for _, p in ey_peers + ez_peers] + [p for _, _, p in rs_peers] + [up, down, right, left]
    for p in peers:
        pl.semaphore_signal(barrier, inc=1, device_id=p, device_id_type=MESH)

    def load(f, row):
        return pltpu.make_async_copy(
            fields.at[f, :, row, :], fld.at[f, row + 2, pl.ds(X0, N + 4), :], load_sem.at[0 if row in faces else 1]
        )

    faces = (0, 1, RY - 2, RY - 1)
    face_loads = [load(f, r) for r in faces for f in range(3)]
    rest_loads = [load(f, r) for r in range(RY) if r not in faces for f in range(3)]
    for cp in face_loads + rest_loads:
        cp.start()
    for cp in face_loads:
        cp.wait()
    pl.semaphore_wait(barrier, len(peers))

    sends = []
    window = pl.ds(XC, N)
    for f in range(3):
        for r in range(2):
            for way, (src, dst, to) in enumerate(((RY + r, r, up), (2 + r, RY + 2 + r, down))):
                slot = way * 6 + f * 2 + r
                sends.append(
                    pltpu.make_async_remote_copy(
                        src_ref=fld.at[f, src, window, :],
                        dst_ref=fld.at[f, dst, window, :],
                        send_sem=halo_send.at[slot],
                        recv_sem=halo_recv.at[slot],
                        device_id=to,
                        device_id_type=MESH,
                    )
                )
    y_halo = list(sends)
    for cp in y_halo:
        cp.start()
    for cp in rest_loads:
        cp.wait()

    lane = lax.broadcasted_iota(jnp.int32, (XB, RZ), 1)
    group = lane // 4
    low_half = lane % 4 < 2

    def pack(b, carry):
        row = pl.multiple_of(XC + b * XB, 8)
        packs = [jnp.zeros((XB, RZ), F32) for _ in range(2)]
        for t in range(3 * RY):
            j = t % 32
            v = fld[t // RY, t % RY + 2, pl.ds(row, XB), :]
            v = pltpu.roll(v, (4 * j + 2) % RZ, 1)
            packs[t // 32] = jnp.where(group == j, v, packs[t // 32])
        out = pl.ds(pl.multiple_of(b * XB, XB), XB)
        pack_r[out, :] = jnp.where(low_half, packs[0], pltpu.roll(packs[1], 2, 1))
        pack_l[out, :] = jnp.where(low_half, pltpu.roll(packs[0], RZ - 2, 1), packs[1])
        return carry

    lax.fori_loop(0, N // XB, pack, 0)
    z_halo = [
        pltpu.make_async_remote_copy(
            src_ref=src,
            dst_ref=dst,
            send_sem=halo_send.at[12 + i],
            recv_sem=halo_recv.at[12 + i],
            device_id=to,
            device_id_type=MESH,
        )
        for i, (src, dst, to) in enumerate(((pack_r, from_left, right), (pack_l, from_right, left)))
    ]
    for cp in z_halo:
        cp.start()
    sends += z_halo

    def split_store(q, row, b, value):
        high = value.astype(BF16)
        cols = pl.ds(pl.multiple_of(row * RZ, RZ), RZ)
        halves[q, pl.ds(b * XB, XB), cols] = high
        halves[q, pl.ds(N + b * XB, XB), cols] = (value - high.astype(F32)).astype(BF16)

    def split_fields(row, carry):
        for f in range(3):
            for b in range(N // XB):
                split_store(f, row, b, fld[f, row + 2, pl.ds(XC + b * XB, XB), :])
        return carry

    lax.fori_loop(0, RY, split_fields, 0)

    eye = lax.broadcasted_iota(jnp.int32, (N, N), 0) == lax.broadcasted_iota(jnp.int32, (N, N), 1)
    below = lax.broadcasted_iota(jnp.int32, (N, N), 0) > lax.broadcasted_iota(jnp.int32, (N, N), 1)

    def gram(q):
        both = halves[q]
        full = lax.dot_general(both, both, (((1,), (1,)), ((), ())), preferred_element_type=F32)
        return full[:N, :N] + full[:N, N:] + full[N:, :N] + full[N:, N:]

    def diagonal(m):
        return jnp.sum(jnp.where(eye, m, 0.0), axis=0, keepdims=True)

    def scatter_store(square, value):
        for o in range(owners):
            piece[o, square * own_rows:(square + 1) * own_rows, :] = value[o * own_rows:(o + 1) * own_rows, :]

    gu, gv, gw = gram(0), gram(1), gram(2)
    scatter_store(0, jnp.where(below, gu, gv))
    diags = [diagonal(m) for m in (gu, gv, gw)]

    def derivative(m2, m1, p1, p2):
        return 8.0 * (p1 - m1) + (m2 - p2)

    def without_z(row, carry):
        for b in range(N // XB):
            at = XC + b * XB

            def dx(f):
                return derivative(*(fld[f, row + 2, pl.ds(at + k, XB), :] for k in (-2, -1, 1, 2)))

            def dy(f):
                return derivative(*(fld[f, row + 2 + k, pl.ds(at, XB), :] for k in (-2, -1, 1, 2)))

            here = pl.ds(b * XB, XB)
            dxu, dxv, dyu, dyv = dx(0), dx(1), dy(0), dy(1)
            rotation, shear = dxv - dyu, dxv + dyu
            enst[row, here, :] = rotation * rotation
            strn[row, here, :] = 2.0 * (dxu * dxu + dyv * dyv) + shear * shear
            dxw_buf[row, here, :] = dx(2)
            dyw_buf[row, here, :] = dy(2)
        return carry

    def with_z(row, carry):
        for b in range(N // XB):
            here = pl.ds(b * XB, XB)

            def dz(f):
                tile = f * RY + row
                shift = lax.rem(RZ + RZ - 2 - 4 * lax.rem(tile, 32), RZ)
                edge = pltpu.roll(merged[0 if f < 2 else 1, here, :], shift, 1)
                v = fld[f, row + 2, pl.ds(XC + b * XB, XB), :]
                m1 = pltpu.roll(jnp.where(lane == RZ - 1, edge, v), 1, 1)
                m2 = pltpu.roll(jnp.where(lane >= RZ - 2, edge, v), 2, 1)
                p1 = pltpu.roll(jnp.where(lane == 0, edge, v), RZ - 1, 1)
                p2 = pltpu.roll(jnp.where(lane < 2, edge, v), RZ - 2, 1)
                return derivative(m2, m1, p1, p2)

            dzu, dzv, dzw = dz(0), dz(1), dz(2)
            dxw, dyw = dxw_buf[row, here, :], dyw_buf[row, here, :]
            r1, r2, s1, s2 = dxw - dzu, dyw - dzv, dxw + dzu, dyw + dzv
            e = (enst[row, here, :] + r1 * r1 + r2 * r2) * (1.0 / 288.0)
            s = (strn[row, here, :] + 2.0 * dzw * dzw + s1 * s1 + s2 * s2) * (1.0 / 288.0)
            enst[row, here, :] = e
            strn[row, here, :] = s
            split_store(3, row, b, e)
            split_store(4, row, b, s)
        return carry

    lax.fori_loop(2, RY - 2, without_z, 0)
    for cp in z_halo:
        cp.wait_recv()

    def merge(b, carry):
        here = pl.ds(pl.multiple_of(b * XB, XB), XB)
        lo, hi = from_left[here, :], from_right[here, :]
        merged[0, here, :] = jnp.where(low_half, lo, pltpu.roll(hi, 2, 1))
        merged[1, here, :] = jnp.where(low_half, pltpu.roll(lo, RZ - 2, 1), hi)
        return carry

    lax.fori_loop(0, N // XB, merge, 0)
    lax.fori_loop(2, RY - 2, with_z, 0)
    for cp in y_halo:
        cp.wait_recv()

    def face_row(i, carry):
        row = i + (RY - 4) * (i // 2)
        without_z(row, 0)
        with_z(row, 0)
        return carry

    lax.fori_loop(0, 4, face_row, 0)
    ge, gs = gram(3), gram(4)
    scatter_store(1, jnp.where(below, gw, gs))
    scatter_store(2, jnp.where(below, ge, 0.0))
    diags += [diagonal(ge), diagonal(gs), jnp.zeros((3, N), F32)]
    tail = jnp.concatenate(diags, axis=0)
    for o in range(owners):
        piece[o, 3 * own_rows:, :] = tail

    def exchange(copies, recv, own):
        for cp in copies:
            cp.start()
        for cp in copies:
            cp.wait_recv()
        total = own
        for k in range(recv.shape[0]):
            total = total + recv[k]
        return total

    rs = [
        pltpu.make_async_remote_copy(
            src_ref=piece.at[o],
            dst_ref=recv_a.at[slot],
            send_sem=rs_send.at[slot],
            recv_sem=rs_recv.at[slot],
            device_id=to,
            device_id_type=MESH,
        )
        for slot, o, to in rs_peers
    ]
    sum_a[...] = exchange(rs, recv_a, piece[me])
    ey = [
        pltpu.make_async_remote_copy(
            src_ref=sum_a,
            dst_ref=recv_b.at[slot],
            send_sem=ey_send.at[slot],
            recv_sem=ey_recv.at[slot],
            device_id=to,
            device_id_type=MESH,
        )
        for slot, to in ey_peers
    ]
    sum_b[...] = exchange(ey, recv_b, sum_a[...])
    ez = [
        pltpu.make_async_remote_copy(
            src_ref=sum_b,
            dst_ref=recv_c.at[slot],
            send_sem=ez_send.at[slot],
            recv_sem=ez_recv.at[slot],
            device_id=to,
            device_id_type=MESH,
        )
        for slot, to in ez_peers
    ]
    total = exchange(ez, recv_c, sum_b[...])

    diag = total[3 * own_rows:, :]
    trace = jnp.sum(diag, axis=1, keepdims=True)
    weight = 1.0 / (5.0 * cells * (trace / (N * cells) + 1e-6))
    weights = [jnp.broadcast_to(weight[q:q + 1, :], (own_rows, N)) for q in range(5)]
    row_id = me * own_rows + lax.broadcasted_iota(jnp.int32, (own_rows, N), 0)
    lower = row_id > lax.broadcasted_iota(jnp.int32, (own_rows, N), 1)
    s0, s1, s2 = (total[q * own_rows:(q + 1) * own_rows, :] for q in range(3))
    w0 = jnp.where(lower, weights[0], weights[1])
    w1 = jnp.where(lower, weights[2], weights[4])
    mine = pl.ds(pl.multiple_of(me * own_rows, own_rows), own_rows)
    comb[mine, :] = s0 * w0 + s1 * w1 + s2 * weights[3]
    ag = [
        pltpu.make_async_remote_copy(
            src_ref=comb.at[mine, :],
            dst_ref=comb.at[mine, :],
            send_sem=ag_send.at[slot],
            recv_sem=ag_recv.at[slot],
            device_id=to,
            device_id_type=MESH,
        )
        for slot, _, to in rs_peers
    ]
    for cp in ag:
        cp.start()
    for cp in sends + rs + ey + ez:
        cp.wait_send()
    five = lax.broadcasted_iota(jnp.int32, diag.shape, 0) < 5
    middle = jnp.sum(jnp.where(five, diag * weight, 0.0), axis=0, keepdims=True)
    for cp in ag:
        cp.wait_recv()
    square = comb[...]
    half = jnp.where(below, square, 0.0) + jnp.where(below, square.T, 0.0)
    cross_out[...] = half + half.T + jnp.where(eye, jnp.broadcast_to(middle, (N, N)), 0.0)
    for cp in ag:
        cp.wait_send()


def split3(v):
    high = v.astype(BF16).astype(F32)
    rest = v - high
    middle = rest.astype(BF16).astype(F32)
    return high, middle, rest - middle


def factor_kernel(cross, e_in, s_in, e_out, s_out, factor, work, upper, out_sem):
    stores = [
        pltpu.make_async_copy(src.at[r], dst.at[:, r, :], out_sem.at[q, r])
        for q, (src, dst) in enumerate(((e_in, e_out), (s_in, s_out)))
        for r in range(RY)
    ]
    for cp in stores:
        cp.start()
    work[...] = cross[...]
    lane = lax.broadcasted_iota(jnp.int32, (8, N), 1)
    sub = lax.broadcasted_iota(jnp.int32, (8, N), 0)
    for p in range(N // 8):
        base = 8 * p
        v = work[base:base + 8, :]
        rows = [jnp.broadcast_to(v[k:k + 1, :], (8, N)) for k in range(8)]
        s = {}
        for k in range(8):
            for m in range(k, 8):
                s[k, m] = jnp.broadcast_to(rows[k][:, base + m:base + m + 1], (8, N))
        panel = None
        for k in range(8):
            r = lax.rsqrt(s[k, k])
            u = {m: s[k, m] * r for m in range(k + 1, 8)}
            for m in range(k + 1, 8):
                for q in range(m, 8):
                    s[m, q] = s[m, q] - u[m] * u[q]
            rows[k] = rows[k] * r
            for m in range(k + 1, 8):
                rows[m] = rows[m] - u[m] * rows[k]
            panel = rows[k] if panel is None else jnp.where(sub == k, rows[k], panel)
        upper[base:base + 8, :] = jnp.where(lane >= sub + base, panel, 0.0)
        if p < N // 8 - 1:
            hi, mid, lo = split3(panel)
            lhs = jnp.concatenate([hi, hi, mid, mid, hi, lo], axis=0).astype(BF16)
            rhs = jnp.concatenate([hi, mid, hi, mid, lo, hi], axis=0).astype(BF16)
            update = lax.dot_general(lhs, rhs, (((0,), (0,)), ((), ())), preferred_element_type=F32)
            work[base + 8:, :] = work[base + 8:, :] - update[base + 8:, :]
    factor[...] = upper[...].T
    for cp in stores:
        cp.wait()


def per_device(sizes, fields):
    gy, gz, zc = sizes
    yc, xc = gy // CORES, gz // zc
    owners = xc * CORES
    rows = 3 * (N // owners) + 8
    vmem = pl.BlockSpec(memory_space=pltpu.VMEM)
    anywhere = pl.BlockSpec(memory_space=pl.ANY)
    hbm = pl.BlockSpec(memory_space=pltpu.HBM)
    grid_rows = jax.ShapeDtypeStruct((RY, N, RZ), F32)
    dma = pltpu.SemaphoreType.DMA

    def body(*refs):
        main_kernel(sizes, *refs)

    e, s, cross = pl.pallas_call(
        body,
        out_shape=(grid_rows, grid_rows, jax.ShapeDtypeStruct((N, N), F32)),
        in_specs=[hbm],
        out_specs=(vmem, vmem, vmem),
        scratch_shapes=[
            pltpu.VMEM((3, RY + 4, N + 16, RZ), F32),
            pltpu.VMEM((N, RZ), F32),
            pltpu.VMEM((N, RZ), F32),
            pltpu.VMEM((N, RZ), F32),
            pltpu.VMEM((N, RZ), F32),
            pltpu.VMEM((2, N, RZ), F32),
            pltpu.VMEM((RY, N, RZ), F32),
            pltpu.VMEM((RY, N, RZ), F32),
            pltpu.VMEM((5, 2 * N, RY * RZ), BF16),
            pltpu.VMEM((owners, rows, N), F32),
            pltpu.VMEM((owners - 1, rows, N), F32),
            pltpu.VMEM((rows, N), F32),
            pltpu.VMEM((yc - 1, rows, N), F32),
            pltpu.VMEM((rows, N), F32),
            pltpu.VMEM((zc - 1, rows, N), F32),
            pltpu.VMEM((N, N), F32),
            dma((2,)),
            dma((14,)),
            dma((14,)),
            dma((owners - 1,)),
            dma((owners - 1,)),
            dma((yc - 1,)),
            dma((yc - 1,)),
            dma((zc - 1,)),
            dma((zc - 1,)),
            dma((owners - 1,)),
            dma((owners - 1,)),
        ],
        compiler_params=pltpu.CompilerParams(collective_id=0, has_side_effects=True, vmem_limit_bytes=48 << 20),
        name="stencil_gram",
    )(pltpu.with_memory_space_constraint(fields, pltpu.HBM))
    whole = jax.ShapeDtypeStruct((N, RY, RZ), F32)
    return pl.pallas_call(
        factor_kernel,
        out_shape=(whole, whole, jax.ShapeDtypeStruct((N, N), F32)),
        in_specs=[vmem, vmem, vmem],
        out_specs=(anywhere, anywhere, vmem),
        scratch_shapes=[
            pltpu.VMEM((N, N), F32),
            pltpu.VMEM((N, N), F32),
            dma((2, RY)),
        ],
        compiler_params=pltpu.CompilerParams(vmem_limit_bytes=16 << 20),
        name="factor",
    )(cross, e, s)


def solution(mesh):
    gy, gz = mesh.shape["gy"], mesh.shape["gz"]
    sizes = (gy, gz, 8 if gz % 8 == 0 else 2)

    def call(fields):
        return per_device(sizes, fields)

    return jax.shard_map(
        call,
        mesh=mesh,
        in_specs=(P(None, None, "gy", "gz"),),
        out_specs=(P(None, "gy", "gz"), P(None, "gy", "gz"), P()),
        check_vma=False,
    )
```

```python
import jax
import jax.numpy as jnp
from jax import lax
from jax.experimental import pallas as pl
from jax.experimental.pallas import tpu as pltpu
from jax.sharding import PartitionSpec as P

MESH = pl.DeviceIdType.MESH
CORES = 2
N = 128
RY = 16
RZ = 128
X0 = 6
XC = X0 + 2
XB = 16
F32 = jnp.float32
BF16 = jnp.bfloat16


def ring_order(count):
    return sorted(range(1, count), key=lambda k: -min(k, count - k))


def main_kernel(
    sizes,
    fields,
    enst,
    strn,
    cross_out,
    fld,
    pack_r,
    pack_l,
    from_left,
    from_right,
    edges,
    dz_buf,
    dxw_buf,
    dyw_buf,
    halves,
    thirds,
    band,
    grams,
    comb,
    load_sem,
    halo_send,
    halo_recv,
    ag_send,
    ag_recv,
    *channels,
):
    gy, gz, zc = sizes
    yc, xc = gy // CORES, gz // zc
    owners = xc * CORES
    own_rows = N // owners
    cells = gy * RY * gz * RZ
    g, h = lax.axis_index("gy"), lax.axis_index("gz")
    y, c = g // CORES, lax.rem(g, CORES)
    x, z = h // zc, lax.rem(h, zc)

    rs_peers = []
    for dx in ring_order(xc) + [0]:
        for dc in range(CORES):
            if dx or dc:
                slot = dx * CORES + dc - 1
                px, pc = lax.rem(x + dx, xc), lax.rem(c + dc, CORES)
                rs_peers.append((slot, px * CORES + pc, (y * CORES + pc, px * zc + z)))
    ey_peers = [(k - 1, (lax.rem(y + k, yc) * CORES + c, h)) for k in ring_order(yc)]
    ez_peers = [(k - 1, (g, x * zc + lax.rem(z + k, zc))) for k in ring_order(zc)]
    me = x * CORES + c
    up, down = (lax.rem(g + 1, gy), h), (lax.rem(g + gy - 1, gy), h)
    right, left = (g, lax.rem(h + 1, gz)), (g, lax.rem(h + gz - 1, gz))

    def remote(src, dst, send, recv, to):
        return pltpu.make_async_remote_copy(
            src_ref=src, dst_ref=dst, send_sem=send, recv_sem=recv, device_id=to, device_id_type=MESH
        )

    def load(row):
        return pltpu.make_async_copy(fields.at[:, :, row, :], fld.at[:, row + 2, pl.ds(X0, N + 4), :], load_sem.at[row])

    faces = (0, 1, RY - 2, RY - 1)
    for row in faces + tuple(range(2, RY - 2)):
        load(row).start()

    barrier = pltpu.get_barrier_semaphore()
    peers = [p for _, p in ey_peers + ez_peers] + [p for _, _, p in rs_peers] + [up, down, right, left]
    for p in peers:
        pl.semaphore_signal(barrier, inc=1, device_id=p, device_id_type=MESH)
    for row in faces:
        load(row).wait()
    pl.semaphore_wait(barrier, len(peers))

    window = pl.ds(XC, N)

    def y_copy(way, r):
        slot = way * 2 + r
        src, dst = 2 + r + (RY - 2) * (1 - way), r + (RY + 2) * way
        to = (lax.rem(g + 1 + (gy - 2) * way, gy), h)
        return remote(
            fld.at[:, src, window, :], fld.at[:, dst, window, :], halo_send.at[slot], halo_recv.at[slot], to
        )

    sends = [y_copy(way, r) for way in range(2) for r in range(2)]
    for cp in sends:
        cp.start()

    def three_way(value):
        high = value.astype(BF16)
        rest = value - high.astype(F32)
        middle = rest.astype(BF16)
        return high, middle, (rest - middle.astype(F32)).astype(BF16)

    def split_fields(row):
        cols = pl.ds(pl.multiple_of(row * RZ, RZ), RZ)
        for f in range(3):
            for b in range(N // XB):
                high, middle, low = three_way(fld[f, row + 2, pl.ds(XC + b * XB, XB), :])
                halves[f, pl.ds(b * XB, XB), cols] = high
                halves[f, pl.ds(N + b * XB, XB), cols] = middle
                thirds[f, pl.ds(b * XB, XB), cols] = low

    def split_face(i, carry):
        split_fields(i + (RY - 4) * (i // 2))
        return carry

    def split_rest(row, carry):
        load(row).wait()
        split_fields(row)
        return carry

    lax.fori_loop(0, 4, split_face, 0)
    lax.fori_loop(2, RY - 2, split_rest, 0)

    lane = lax.broadcasted_iota(jnp.int32, (XB, RZ), 1)
    group = lane // 4
    member = lane % 4
    low_half = member < 2

    def pack(b, carry):
        row = pl.multiple_of(XC + b * XB, 8)
        packs = [jnp.zeros((XB, RZ), F32) for _ in range(2)]
        for t in range(3 * RY):
            j = t % 32
            v = fld[t // RY, t % RY + 2, pl.ds(row, XB), :]
            v = pltpu.roll(v, (4 * j + 2) % RZ, 1)
            packs[t // 32] = jnp.where(group == j, v, packs[t // 32])
        out = pl.ds(pl.multiple_of(b * XB, XB), XB)
        pack_r[out, :] = jnp.where(low_half, packs[0], pltpu.roll(packs[1], 2, 1))
        pack_l[out, :] = jnp.where(low_half, pltpu.roll(packs[0], RZ - 2, 1), packs[1])
        return carry

    lax.fori_loop(0, N // XB, pack, 0)
    z_halo = [
        remote(pack_r, from_left, halo_send.at[4], halo_recv.at[4], right),
        remote(pack_l, from_right, halo_send.at[5], halo_recv.at[5], left),
    ]
    for cp in z_halo:
        cp.start()
    sends += z_halo

    eye = lax.broadcasted_iota(jnp.int32, (N, N), 0) == lax.broadcasted_iota(jnp.int32, (N, N), 1)
    below = lax.broadcasted_iota(jnp.int32, (N, N), 0) > lax.broadcasted_iota(jnp.int32, (N, N), 1)

    def gram(q, cols):
        both = halves[q, :, cols]
        full = lax.dot_general(both, both, (((1,), (1,)), ((), ())), preferred_element_type=F32)
        return full[:N, :N] + full[:N, N:] + full[N:, :N] + full[N:, N:]

    def diagonal(m):
        return jnp.sum(jnp.where(eye, m, 0.0), axis=0, keepdims=True)

    def fill(piece, squares, diags):
        tail = jnp.concatenate(diags + [jnp.zeros((8 - len(diags), N), F32)], axis=0)
        for o in range(owners):
            for k, value in enumerate(squares):
                piece[o, k * own_rows:(k + 1) * own_rows, :] = value[o * own_rows:(o + 1) * own_rows, :]
            piece[o, len(squares) * own_rows:, :] = tail

    class Channel:
        def __init__(self, piece, recv_a, sum_a, recv_b, sum_b, recv_c, rs_s, rs_r, ey_s, ey_r, ez_s, ez_r):
            self.piece, self.recv_a, self.sum_a = piece, recv_a, sum_a
            self.recv_b, self.sum_b, self.recv_c = recv_b, sum_b, recv_c
            self.rs = [remote(piece.at[o], recv_a.at[k], rs_s.at[k], rs_r.at[k], to) for k, o, to in rs_peers]
            self.ey = [remote(sum_a, recv_b.at[k], ey_s.at[k], ey_r.at[k], to) for k, to in ey_peers]
            self.ez = [remote(sum_b, recv_c.at[k], ez_s.at[k], ez_r.at[k], to) for k, to in ez_peers]

        def start(self, copies):
            for cp in copies:
                cp.start()

        def collect(self, copies, recv, own):
            for cp in copies:
                cp.wait_recv()
            for k in range(recv.shape[0]):
                own = own + recv[k]
            return own

        def scatter(self):
            self.start(self.rs)

        def along_y(self):
            self.sum_a[...] = self.collect(self.rs, self.recv_a, self.piece[me])
            self.start(self.ey)

        def along_z(self):
            self.sum_b[...] = self.collect(self.ey, self.recv_b, self.sum_a[...])
            self.start(self.ez)

        def total(self):
            return self.collect(self.ez, self.recv_c, self.sum_b[...])

    early, late = Channel(*channels[:12]), Channel(*channels[12:])
    everything = pl.ds(0, RY * RZ)
    gu, gv, gw = (gram(f, everything) for f in range(3))
    fill(early.piece, [jnp.where(below, gu, gv), gw], [diagonal(m) for m in (gu, gv, gw)])
    early.scatter()

    wide = 2 * RZ
    depth = lax.broadcasted_iota(jnp.int32, (3 * wide, wide), 0) % wide
    column = lax.broadcasted_iota(jnp.int32, (3 * wide, wide), 1)
    step = jnp.where(depth // RZ == column // RZ, column - depth, 0)
    weights = jnp.where(step == 2, 1.0, 0.0) - jnp.where(step == -2, 1.0, 0.0)
    weights = weights + jnp.where(step == -1, 8.0, 0.0) - jnp.where(step == 1, 8.0, 0.0)
    band[...] = weights.astype(BF16)

    def inner_z(pair):
        cols = pl.ds(pl.multiple_of(pair * wide, wide), wide)
        parts = [
            jnp.concatenate([ref[f, first:first + N, cols] for f in range(3)], axis=0)
            for ref, first in ((halves, 0), (halves, N), (thirds, 0))
        ]
        out = lax.dot_general(
            jnp.concatenate(parts, axis=1), band[...], (((1,), (0,)), ((), ())), preferred_element_type=F32
        )
        for f in range(3):
            for r in range(2):
                dz_buf[f, 2 * pair + r] = out[f * N:(f + 1) * N, r * RZ:(r + 1) * RZ]

    def derivative(m2, m1, p1, p2):
        return 8.0 * (p1 - m1) + (m2 - p2)

    def without_z(row):
        for b in range(N // XB):
            at = XC + b * XB

            def dx(f):
                return derivative(*(fld[f, row + 2, pl.ds(at + k, XB), :] for k in (-2, -1, 1, 2)))

            def dy(f):
                return derivative(*(fld[f, row + 2 + k, pl.ds(at, XB), :] for k in (-2, -1, 1, 2)))

            here = pl.ds(b * XB, XB)
            dxu, dxv, dyu, dyv = dx(0), dx(1), dy(0), dy(1)
            rotation, shear = dxv - dyu, dxv + dyu
            enst[row, here, :] = rotation * rotation
            strn[row, here, :] = 2.0 * (dxu * dxu + dyv * dyv) + shear * shear
            dxw_buf[row, here, :] = dx(2)
            dyw_buf[row, here, :] = dy(2)

    outer = (lane < 2) | (lane >= RZ - 2)

    def with_z(row):
        cols = pl.ds(pl.multiple_of(row * RZ, RZ), RZ)
        for b in range(N // XB):
            here = pl.ds(b * XB, XB)

            def dz(f):
                shift = lax.rem(RZ + RZ - 2 - 4 * lax.rem(f * RY + row, 32), RZ)
                edge = pltpu.roll(edges[0 if f < 2 else 1, here, :], shift, 1)
                return dz_buf[f, row, here, :] + jnp.where(outer, edge, 0.0)

            dzu, dzv, dzw = dz(0), dz(1), dz(2)
            dxw, dyw = dxw_buf[row, here, :], dyw_buf[row, here, :]
            r1, r2, s1, s2 = dxw - dzu, dyw - dzv, dxw + dzu, dyw + dzv
            e = (enst[row, here, :] + r1 * r1 + r2 * r2) * (1.0 / 288.0)
            s = (strn[row, here, :] + 2.0 * dzw * dzw + s1 * s1 + s2 * s2) * (1.0 / 288.0)
            enst[row, here, :] = e
            strn[row, here, :] = s
            for q, value in ((3, e), (4, s)):
                high = value.astype(BF16)
                halves[q, here, cols] = high
                halves[q, pl.ds(N + b * XB, XB), cols] = (value - high.astype(F32)).astype(BF16)

    def inner_pair(pair, carry):
        inner_z(pair)
        without_z(2 * pair)
        without_z(2 * pair + 1)
        return carry

    def face_pair(i, carry):
        inner_z(i * (RY // 2 - 1))
        return carry

    lax.fori_loop(1, RY // 2 - 1, inner_pair, 0)
    lax.fori_loop(0, 2, face_pair, 0)
    for cp in z_halo:
        cp.wait_recv()

    def edge(b, carry):
        here = pl.ds(pl.multiple_of(b * XB, XB), XB)
        lo, hi = from_left[here, :], from_right[here, :]
        packs = (
            jnp.where(low_half, lo, pltpu.roll(hi, 2, 1)),
            jnp.where(low_half, pltpu.roll(lo, RZ - 2, 1), hi),
        )
        for k, m in enumerate(packs):
            next2, next1 = pltpu.roll(m, RZ - 2, 1), pltpu.roll(m, RZ - 1, 1)
            last1, last2 = pltpu.roll(m, 1, 1), pltpu.roll(m, 2, 1)
            tops = jnp.where(member == 0, -next2, 8.0 * next1 - next2)
            bottoms = jnp.where(member == 2, last2 - 8.0 * last1, last2)
            edges[k, here, :] = jnp.where(low_half, tops, bottoms)
        return carry

    lax.fori_loop(0, N // XB, edge, 0)

    def inner_row(row, carry):
        with_z(row)
        return carry

    lax.fori_loop(2, RY - 2, inner_row, 0)
    inside = pl.ds(2 * RZ, (RY - 4) * RZ)
    for q in range(2):
        grams[q] = gram(3 + q, inside)

    def face(which):
        first = (RY - 2) * which
        for r in range(2):
            y_copy(which, r).wait_recv()

        def face_row(r, carry):
            without_z(first + r)
            with_z(first + r)
            return carry

        lax.fori_loop(0, 2, face_row, 0)
        cols = pl.ds(pl.multiple_of(first * RZ, wide), wide)
        for q in range(2):
            grams[q] = grams[q] + gram(3 + q, cols)

    def one_face(i, carry):
        face(lax.rem(i + 1 + c, CORES))
        return carry

    lax.fori_loop(0, 2, one_face, 0)

    ge, gs = grams[0], grams[1]
    fill(late.piece, [jnp.where(below, ge, gs)], [diagonal(ge), diagonal(gs)])
    late.scatter()
    early.along_y()
    late.along_y()
    early.along_z()
    late.along_z()
    first_sums = early.total()
    last_sums = late.total()

    diag = jnp.concatenate(
        [first_sums[2 * own_rows:2 * own_rows + 3, :], last_sums[own_rows:own_rows + 5, :]], axis=0
    )
    trace = jnp.sum(diag, axis=1, keepdims=True)
    weight = 1.0 / (5.0 * cells * (trace / (N * cells) + 1e-6))
    wide_weights = [jnp.broadcast_to(weight[q:q + 1, :], (own_rows, N)) for q in range(5)]
    row_id = me * own_rows + lax.broadcasted_iota(jnp.int32, (own_rows, N), 0)
    lower = row_id > lax.broadcasted_iota(jnp.int32, (own_rows, N), 1)
    mine = pl.ds(pl.multiple_of(me * own_rows, own_rows), own_rows)
    comb[mine, :] = (
        first_sums[:own_rows, :] * jnp.where(lower, wide_weights[0], wide_weights[1])
        + first_sums[own_rows:2 * own_rows, :] * jnp.where(lower, wide_weights[2], 0.0)
        + last_sums[:own_rows, :] * jnp.where(lower, wide_weights[3], wide_weights[4])
    )
    ag = [remote(comb.at[mine, :], comb.at[mine, :], ag_send.at[k], ag_recv.at[k], to) for k, _, to in rs_peers]
    for cp in ag:
        cp.start()
    for cp in sends + early.rs + early.ey + early.ez + late.rs + late.ey + late.ez:
        cp.wait_send()
    five = lax.broadcasted_iota(jnp.int32, diag.shape, 0) < 5
    middle = jnp.sum(jnp.where(five, diag * weight, 0.0), axis=0, keepdims=True)
    for cp in ag:
        cp.wait_recv()
    square = comb[...]
    half = jnp.where(below, square, 0.0) + jnp.where(below, square.T, 0.0)
    cross_out[...] = half + half.T + jnp.where(eye, jnp.broadcast_to(middle, (N, N)), 0.0)
    for cp in ag:
        cp.wait_send()


def split3(v):
    high = v.astype(BF16).astype(F32)
    rest = v - high
    middle = rest.astype(BF16).astype(F32)
    return high, middle, rest - middle


def factor_kernel(cross, e_in, s_in, e_out, s_out, factor, work, upper, out_sem):
    stores = [
        pltpu.make_async_copy(src.at[r], dst.at[:, r, :], out_sem.at[q, r])
        for q, (src, dst) in enumerate(((e_in, e_out), (s_in, s_out)))
        for r in range(RY)
    ]
    for cp in stores:
        cp.start()
    work[...] = cross[...]
    lane = lax.broadcasted_iota(jnp.int32, (8, N), 1)
    sub = lax.broadcasted_iota(jnp.int32, (8, N), 0)
    for p in range(N // 8):
        base = 8 * p
        v = work[base:base + 8, :]
        rows = [jnp.broadcast_to(v[k:k + 1, :], (8, N)) for k in range(8)]
        s = {}
        for k in range(8):
            for m in range(k, 8):
                s[k, m] = jnp.broadcast_to(rows[k][:, base + m:base + m + 1], (8, N))
        panel = None
        for k in range(8):
            r = lax.rsqrt(s[k, k])
            u = {m: s[k, m] * r for m in range(k + 1, 8)}
            for m in range(k + 1, 8):
                for q in range(m, 8):
                    s[m, q] = s[m, q] - u[m] * u[q]
            rows[k] = rows[k] * r
            for m in range(k + 1, 8):
                rows[m] = rows[m] - u[m] * rows[k]
            panel = rows[k] if panel is None else jnp.where(sub == k, rows[k], panel)
        upper[base:base + 8, :] = jnp.where(lane >= sub + base, panel, 0.0)
        if p < N // 8 - 1:
            hi, mid, lo = split3(panel)
            lhs = jnp.concatenate([hi, hi, mid, mid, hi, lo], axis=0).astype(BF16)
            rhs = jnp.concatenate([hi, mid, hi, mid, lo, hi], axis=0).astype(BF16)
            update = lax.dot_general(lhs, rhs, (((0,), (0,)), ((), ())), preferred_element_type=F32)
            work[base + 8:, :] = work[base + 8:, :] - update[base + 8:, :]
    factor[...] = upper[...].T
    for cp in stores:
        cp.wait()


def per_device(sizes, fields):
    gy, gz, zc = sizes
    yc, xc = gy // CORES, gz // zc
    owners = xc * CORES
    vmem = pl.BlockSpec(memory_space=pltpu.VMEM)
    anywhere = pl.BlockSpec(memory_space=pl.ANY)
    grid_rows = jax.ShapeDtypeStruct((RY, N, RZ), F32)
    dma = pltpu.SemaphoreType.DMA

    def body(*refs):
        main_kernel(sizes, *refs)

    def channel(squares):
        rows = squares * (N // owners) + 8
        return [
            pltpu.VMEM((owners, rows, N), F32),
            pltpu.VMEM((owners - 1, rows, N), F32),
            pltpu.VMEM((rows, N), F32),
            pltpu.VMEM((yc - 1, rows, N), F32),
            pltpu.VMEM((rows, N), F32),
            pltpu.VMEM((zc - 1, rows, N), F32),
            dma((owners - 1,)),
            dma((owners - 1,)),
            dma((yc - 1,)),
            dma((yc - 1,)),
            dma((zc - 1,)),
            dma((zc - 1,)),
        ]

    e, s, cross = pl.pallas_call(
        body,
        out_shape=(grid_rows, grid_rows, jax.ShapeDtypeStruct((N, N), F32)),
        in_specs=[pl.BlockSpec(memory_space=pltpu.HBM)],
        out_specs=(vmem, vmem, vmem),
        scratch_shapes=[
            pltpu.VMEM((3, RY + 4, N + 16, RZ), F32),
            pltpu.VMEM((N, RZ), F32),
            pltpu.VMEM((N, RZ), F32),
            pltpu.VMEM((N, RZ), F32),
            pltpu.VMEM((N, RZ), F32),
            pltpu.VMEM((2, N, RZ), F32),
            pltpu.VMEM((3, RY, N, RZ), F32),
            pltpu.VMEM((RY, N, RZ), F32),
            pltpu.VMEM((RY, N, RZ), F32),
            pltpu.VMEM((5, 2 * N, RY * RZ), BF16),
            pltpu.VMEM((3, N, RY * RZ), BF16),
            pltpu.VMEM((6 * RZ, 2 * RZ), BF16),
            pltpu.VMEM((2, N, N), F32),
            pltpu.VMEM((N, N), F32),
            dma((RY,)),
            dma((6,)),
            dma((6,)),
            dma((owners - 1,)),
            dma((owners - 1,)),
            *channel(2),
            *channel(1),
        ],
        compiler_params=pltpu.CompilerParams(collective_id=0, has_side_effects=True, vmem_limit_bytes=48 << 20),
        name="stencil_gram",
    )(pltpu.with_memory_space_constraint(fields, pltpu.HBM))
    whole = jax.ShapeDtypeStruct((N, RY, RZ), F32)
    return pl.pallas_call(
        factor_kernel,
        out_shape=(whole, whole, jax.ShapeDtypeStruct((N, N), F32)),
        in_specs=[vmem, vmem, vmem],
        out_specs=(anywhere, anywhere, vmem),
        scratch_shapes=[
            pltpu.VMEM((N, N), F32),
            pltpu.VMEM((N, N), F32),
            dma((2, RY)),
        ],
        compiler_params=pltpu.CompilerParams(vmem_limit_bytes=16 << 20),
        name="factor",
    )(cross, e, s)


def solution(mesh):
    gy, gz = mesh.shape["gy"], mesh.shape["gz"]
    sizes = (gy, gz, 8 if gz % 8 == 0 else 2)

    def call(fields):
        return per_device(sizes, fields)

    return jax.shard_map(
        call,
        mesh=mesh,
        in_specs=(P(None, None, "gy", "gz"),),
        out_specs=(P(None, "gy", "gz"), P(None, "gy", "gz"), P()),
        check_vma=False,
    )
```

```python
import jax
import jax.numpy as jnp
from jax import lax
from jax.experimental import pallas as pl
from jax.experimental.pallas import tpu as pltpu
from jax.sharding import PartitionSpec as P

MESH = pl.DeviceIdType.MESH
CORES = 2
N = 128
RY = 16
RZ = 128
X0 = 6
XC = X0 + 2
XB = 16
PARTS = 2
F32 = jnp.float32
BF16 = jnp.bfloat16


def ring_order(count):
    return sorted(range(1, count), key=lambda k: -min(k, count - k))


def main_kernel(
    sizes,
    fields,
    enst,
    strn,
    cross_out,
    fld,
    pack_r,
    pack_l,
    from_left,
    from_right,
    edges,
    dz_buf,
    dxw_buf,
    dyw_buf,
    halves,
    thirds,
    band,
    grams,
    comb,
    load_sem,
    halo_send,
    halo_recv,
    ag_send,
    ag_recv,
    *channels,
):
    gy, gz, zc = sizes
    yc, xc = gy // CORES, gz // zc
    owners = xc * CORES
    own_rows = N // owners
    cells = gy * RY * gz * RZ
    g, h = lax.axis_index("gy"), lax.axis_index("gz")
    y, c = g // CORES, lax.rem(g, CORES)
    x, z = h // zc, lax.rem(h, zc)

    rs_peers = []
    for dx in ring_order(xc) + [0]:
        for dc in range(CORES):
            if dx or dc:
                slot = dx * CORES + dc - 1
                px, pc = lax.rem(x + dx, xc), lax.rem(c + dc, CORES)
                rs_peers.append((slot, px * CORES + pc, (y * CORES + pc, px * zc + z)))
    ey_peers = [(k - 1, (lax.rem(y + k, yc) * CORES + c, h)) for k in ring_order(yc)]
    ez_peers = [(k - 1, (g, x * zc + lax.rem(z + k, zc))) for k in ring_order(zc)]
    me = x * CORES + c
    up, down = (lax.rem(g + 1, gy), h), (lax.rem(g + gy - 1, gy), h)
    right, left = (g, lax.rem(h + 1, gz)), (g, lax.rem(h + gz - 1, gz))

    def remote(src, dst, send, recv, to):
        return pltpu.make_async_remote_copy(
            src_ref=src, dst_ref=dst, send_sem=send, recv_sem=recv, device_id=to, device_id_type=MESH
        )

    def load(row):
        return pltpu.make_async_copy(fields.at[:, :, row, :], fld.at[:, row + 2, pl.ds(X0, N + 4), :], load_sem.at[row])

    faces = (0, 1, RY - 2, RY - 1)
    for row in faces + tuple(range(2, RY - 2)):
        load(row).start()

    barrier = pltpu.get_barrier_semaphore()
    peers = [p for _, p in ey_peers + ez_peers] + [p for _, _, p in rs_peers] + [up, down, right, left]
    for p in peers:
        pl.semaphore_signal(barrier, inc=1, device_id=p, device_id_type=MESH)
    for row in faces:
        load(row).wait()
    pl.semaphore_wait(barrier, len(peers))

    window = pl.ds(XC, N)

    def y_copy(way, r):
        slot = way * 2 + r
        src, dst = 2 + r + (RY - 2) * (1 - way), r + (RY + 2) * way
        to = (lax.rem(g + 1 + (gy - 2) * way, gy), h)
        return remote(
            fld.at[:, src, window, :], fld.at[:, dst, window, :], halo_send.at[slot], halo_recv.at[slot], to
        )

    sends = [y_copy(way, r) for way in range(2) for r in range(2)]
    for cp in sends:
        cp.start()

    def three_way(value):
        high = value.astype(BF16)
        rest = value - high.astype(F32)
        middle = rest.astype(BF16)
        return high, middle, (rest - middle.astype(F32)).astype(BF16)

    def split_fields(row):
        cols = pl.ds(pl.multiple_of(row * RZ, RZ), RZ)
        for f in range(3):
            for b in range(N // XB):
                high, middle, low = three_way(fld[f, row + 2, pl.ds(XC + b * XB, XB), :])
                halves[f, pl.ds(b * XB, XB), cols] = high
                halves[f, pl.ds(N + b * XB, XB), cols] = middle
                thirds[f, pl.ds(b * XB, XB), cols] = low

    def split_face(i, carry):
        split_fields(i + (RY - 4) * (i // 2))
        return carry

    def split_rest(row, carry):
        load(row).wait()
        split_fields(row)
        return carry

    lax.fori_loop(0, 4, split_face, 0)
    lax.fori_loop(2, RY - 2, split_rest, 0)

    lane = lax.broadcasted_iota(jnp.int32, (XB, RZ), 1)
    group = lane // 4
    member = lane % 4
    low_half = member < 2

    def pack(b, carry):
        row = pl.multiple_of(XC + b * XB, 8)
        packs = [jnp.zeros((XB, RZ), F32) for _ in range(2)]
        for t in range(3 * RY):
            j = t % 32
            v = fld[t // RY, t % RY + 2, pl.ds(row, XB), :]
            v = pltpu.roll(v, (4 * j + 2) % RZ, 1)
            packs[t // 32] = jnp.where(group == j, v, packs[t // 32])
        out = pl.ds(pl.multiple_of(b * XB, XB), XB)
        pack_r[out, :] = jnp.where(low_half, packs[0], pltpu.roll(packs[1], 2, 1))
        pack_l[out, :] = jnp.where(low_half, pltpu.roll(packs[0], RZ - 2, 1), packs[1])
        return carry

    lax.fori_loop(0, N // XB, pack, 0)
    z_halo = [
        remote(pack_r, from_left, halo_send.at[4], halo_recv.at[4], right),
        remote(pack_l, from_right, halo_send.at[5], halo_recv.at[5], left),
    ]
    for cp in z_halo:
        cp.start()
    sends += z_halo

    eye = lax.broadcasted_iota(jnp.int32, (N, N), 0) == lax.broadcasted_iota(jnp.int32, (N, N), 1)
    below = lax.broadcasted_iota(jnp.int32, (N, N), 0) > lax.broadcasted_iota(jnp.int32, (N, N), 1)

    def gram(q, cols):
        both = halves[q, :, cols]
        full = lax.dot_general(both, both, (((1,), (1,)), ((), ())), preferred_element_type=F32)
        return full[:N, :N] + full[:N, N:] + full[N:, :N] + full[N:, N:]

    def diagonal(m):
        return jnp.sum(jnp.where(eye, m, 0.0), axis=0, keepdims=True)

    def fill(piece, squares, diags):
        tail = jnp.concatenate(diags, axis=0)
        for o in range(owners):
            for k, value in enumerate(squares):
                piece[o, k * own_rows:(k + 1) * own_rows, :] = value[o * own_rows:(o + 1) * own_rows, :]
            piece[o, len(squares) * own_rows:, :] = tail

    class Channel:
        def __init__(self, piece, recv_a, sum_a, recv_b, sum_b, recv_c, rs_s, rs_r, ey_s, ey_r, ez_s, ez_r):
            self.piece, self.recv_a, self.sum_a = piece, recv_a, sum_a
            self.recv_b, self.sum_b, self.recv_c = recv_b, sum_b, recv_c
            self.rs = [remote(piece.at[o], recv_a.at[k], rs_s.at[k], rs_r.at[k], to) for k, o, to in rs_peers]
            self.ey = [remote(sum_a, recv_b.at[k], ey_s.at[k], ey_r.at[k], to) for k, to in ey_peers]
            self.ez = [remote(sum_b, recv_c.at[k], ez_s.at[k], ez_r.at[k], to) for k, to in ez_peers]

        def start(self, copies):
            for cp in copies:
                cp.start()

        def collect(self, copies, recv, own):
            for cp in copies:
                cp.wait_recv()
            for k in range(recv.shape[0]):
                own = own + recv[k]
            return own

        def scatter(self):
            self.start(self.rs)

        def along_y(self):
            self.sum_a[...] = self.collect(self.rs, self.recv_a, self.piece[me])
            self.start(self.ey)

        def along_z(self):
            self.sum_b[...] = self.collect(self.ey, self.recv_b, self.sum_a[...])
            self.start(self.ez)

        def total(self):
            return self.collect(self.ez, self.recv_c, self.sum_b[...])

    early, late = Channel(*channels[:12]), Channel(*channels[12:])
    everything = pl.ds(0, RY * RZ)
    gu, gv, gw = (gram(f, everything) for f in range(3))
    fill(early.piece, [jnp.where(below, gu, gv), gw], [diagonal(m) for m in (gu, gv, gw)])
    early.scatter()

    wide = 2 * RZ
    step = lax.broadcasted_iota(jnp.int32, (RZ, RZ), 1) - lax.broadcasted_iota(jnp.int32, (RZ, RZ), 0)
    weights = jnp.where(step == 2, 1.0, jnp.where(step == -2, -1.0, 0.0))
    weights = jnp.where(step == -1, 8.0, jnp.where(step == 1, -8.0, weights)).astype(BF16)
    band[...] = jnp.zeros_like(band)
    band[:RZ, :RZ] = weights
    band[RZ:, RZ:] = weights

    def inner_z(pair, part):
        rows = N // PARTS
        cols = pl.ds(pl.multiple_of(pair * wide, wide), wide)
        at = part * rows
        parts = [
            ref[f, pl.ds(first + at, rows), cols]
            for ref, first in ((halves, 0), (halves, N), (thirds, 0))
            for f in range(3)
        ]
        out = lax.dot_general(
            jnp.concatenate(parts, axis=0), band[...], (((1,), (0,)), ((), ())), preferred_element_type=F32
        )
        for f in range(3):
            for r in range(2):
                a, b, c2 = (out[(3 * k + f) * rows:(3 * k + f + 1) * rows, r * RZ:(r + 1) * RZ] for k in range(3))
                dz_buf[f, 2 * pair + r, pl.ds(at, rows), :] = a + b + c2

    def derivative(m2, m1, p1, p2):
        return 8.0 * (p1 - m1) + (m2 - p2)

    def without_z(row, blocks=range(N // XB)):
        for b in blocks:
            at = XC + b * XB

            def dx(f):
                return derivative(*(fld[f, row + 2, pl.ds(at + k, XB), :] for k in (-2, -1, 1, 2)))

            def dy(f):
                return derivative(*(fld[f, row + 2 + k, pl.ds(at, XB), :] for k in (-2, -1, 1, 2)))

            here = pl.ds(b * XB, XB)
            dxu, dxv, dyu, dyv = dx(0), dx(1), dy(0), dy(1)
            rotation, shear = dxv - dyu, dxv + dyu
            enst[row, here, :] = rotation * rotation
            strn[row, here, :] = 2.0 * (dxu * dxu + dyv * dyv) + shear * shear
            dxw_buf[row, here, :] = dx(2)
            dyw_buf[row, here, :] = dy(2)

    outer = (lane < 2) | (lane >= RZ - 2)

    def with_z(row):
        cols = pl.ds(pl.multiple_of(row * RZ, RZ), RZ)
        for b in range(N // XB):
            here = pl.ds(b * XB, XB)

            def dz(f):
                shift = lax.rem(RZ + RZ - 2 - 4 * lax.rem(f * RY + row, 32), RZ)
                edge = pltpu.roll(edges[0 if f < 2 else 1, here, :], shift, 1)
                return dz_buf[f, row, here, :] + jnp.where(outer, edge, 0.0)

            dzu, dzv, dzw = dz(0), dz(1), dz(2)
            dxw, dyw = dxw_buf[row, here, :], dyw_buf[row, here, :]
            r1, r2, s1, s2 = dxw - dzu, dyw - dzv, dxw + dzu, dyw + dzv
            e = (enst[row, here, :] + r1 * r1 + r2 * r2) * (1.0 / 288.0)
            s = (strn[row, here, :] + 2.0 * dzw * dzw + s1 * s1 + s2 * s2) * (1.0 / 288.0)
            enst[row, here, :] = e
            strn[row, here, :] = s
            for q, value in ((3, e), (4, s)):
                high = value.astype(BF16)
                halves[q, here, cols] = high
                halves[q, pl.ds(N + b * XB, XB), cols] = (value - high.astype(F32)).astype(BF16)

    def inner_pair(pair, carry):
        each = N // XB // PARTS
        for part in range(PARTS):
            inner_z(pair, part)
            for r in range(2):
                without_z(2 * pair + r, range(part * each, (part + 1) * each))
        return carry

    def face_pair(i, carry):
        for part in range(PARTS):
            inner_z(i * (RY // 2 - 1), part)
        return carry

    lax.fori_loop(1, RY // 2 - 1, inner_pair, 0)
    lax.fori_loop(0, 2, face_pair, 0)
    for cp in z_halo:
        cp.wait_recv()

    def edge(b, carry):
        here = pl.ds(pl.multiple_of(b * XB, XB), XB)
        lo, hi = from_left[here, :], from_right[here, :]
        packs = (
            jnp.where(low_half, lo, pltpu.roll(hi, 2, 1)),
            jnp.where(low_half, pltpu.roll(lo, RZ - 2, 1), hi),
        )
        for k, m in enumerate(packs):
            next2, next1 = pltpu.roll(m, RZ - 2, 1), pltpu.roll(m, RZ - 1, 1)
            last1, last2 = pltpu.roll(m, 1, 1), pltpu.roll(m, 2, 1)
            tops = jnp.where(member == 0, -next2, 8.0 * next1 - next2)
            bottoms = jnp.where(member == 2, last2 - 8.0 * last1, last2)
            edges[k, here, :] = jnp.where(low_half, tops, bottoms)
        return carry

    lax.fori_loop(0, N // XB, edge, 0)

    def inner_rows(pair, carry):
        with_z(2 * pair)
        with_z(2 * pair + 1)
        return carry

    lax.fori_loop(1, RY // 2 - 1, inner_rows, 0)
    inside = pl.ds(2 * RZ, (RY - 4) * RZ)
    for q in range(2):
        grams[q] = gram(3 + q, inside)

    def face(which):
        first = (RY - 2) * which
        for r in range(2):
            y_copy(which, r).wait_recv()

        def face_row(r, carry):
            without_z(first + r)
            with_z(first + r)
            return carry

        lax.fori_loop(0, 2, face_row, 0)
        cols = pl.ds(pl.multiple_of(first * RZ, wide), wide)
        for q in range(2):
            grams[q] = grams[q] + gram(3 + q, cols)

    face(lax.rem(1 + c, CORES))
    early.along_y()
    face(c)

    ge, gs = grams[0], grams[1]
    fill(late.piece, [jnp.where(below, ge, gs)], [diagonal(ge), diagonal(gs)])
    late.scatter()
    late.along_y()
    early.along_z()
    late.along_z()
    first_sums = early.total()
    last_sums = late.total()

    diag = jnp.concatenate([first_sums[2 * own_rows:, :], last_sums[own_rows:, :]], axis=0)
    trace = jnp.sum(diag, axis=1, keepdims=True)
    weight = 1.0 / (5.0 * cells * (trace / (N * cells) + 1e-6))
    wide_weights = [jnp.broadcast_to(weight[q:q + 1, :], (own_rows, N)) for q in range(5)]
    row_id = me * own_rows + lax.broadcasted_iota(jnp.int32, (own_rows, N), 0)
    lower = row_id > lax.broadcasted_iota(jnp.int32, (own_rows, N), 1)
    mine = pl.ds(pl.multiple_of(me * own_rows, own_rows), own_rows)
    comb[mine, :] = (
        first_sums[:own_rows, :] * jnp.where(lower, wide_weights[0], wide_weights[1])
        + first_sums[own_rows:2 * own_rows, :] * jnp.where(lower, wide_weights[2], 0.0)
        + last_sums[:own_rows, :] * jnp.where(lower, wide_weights[3], wide_weights[4])
    )
    ag = [remote(comb.at[mine, :], comb.at[mine, :], ag_send.at[k], ag_recv.at[k], to) for k, _, to in rs_peers]
    for cp in ag:
        cp.start()
    for cp in sends + early.rs + early.ey + early.ez + late.rs + late.ey + late.ez:
        cp.wait_send()
    middle = jnp.sum(diag * weight, axis=0, keepdims=True)
    for cp in ag:
        cp.wait_recv()
    square = comb[...]
    half = jnp.where(below, square, 0.0) + jnp.where(below, square.T, 0.0)
    cross_out[...] = half + half.T + jnp.where(eye, jnp.broadcast_to(middle, (N, N)), 0.0)
    for cp in ag:
        cp.wait_send()


def split3(v):
    high = v.astype(BF16).astype(F32)
    rest = v - high
    middle = rest.astype(BF16).astype(F32)
    return high, middle, rest - middle


def factor_kernel(cross, e_in, s_in, e_out, s_out, factor, work, upper, out_sem):
    stores = [
        pltpu.make_async_copy(src.at[r], dst.at[:, r, :], out_sem.at[q, r])
        for q, (src, dst) in enumerate(((e_in, e_out), (s_in, s_out)))
        for r in range(RY)
    ]
    for cp in stores:
        cp.start()
    work[...] = cross[...]
    lane = lax.broadcasted_iota(jnp.int32, (8, N), 1)
    sub = lax.broadcasted_iota(jnp.int32, (8, N), 0)
    for p in range(N // 8):
        base = 8 * p
        v = work[base:base + 8, :]
        rows = [jnp.broadcast_to(v[k:k + 1, :], (8, N)) for k in range(8)]
        s = {}
        for k in range(8):
            for m in range(k, 8):
                s[k, m] = jnp.broadcast_to(rows[k][:, base + m:base + m + 1], (8, N))
        panel = None
        for k in range(8):
            r = lax.rsqrt(s[k, k])
            u = {m: s[k, m] * r for m in range(k + 1, 8)}
            for m in range(k + 1, 8):
                for q in range(m, 8):
                    s[m, q] = s[m, q] - u[m] * u[q]
            rows[k] = rows[k] * r
            for m in range(k + 1, 8):
                rows[m] = rows[m] - u[m] * rows[k]
            panel = rows[k] if panel is None else jnp.where(sub == k, rows[k], panel)
        upper[base:base + 8, :] = jnp.where(lane >= sub + base, panel, 0.0)
        if p < N // 8 - 1:
            hi, mid, lo = split3(panel)
            lhs = jnp.concatenate([hi, hi, mid, mid, hi, lo], axis=0).astype(BF16)
            rhs = jnp.concatenate([hi, mid, hi, mid, lo, hi], axis=0).astype(BF16)
            update = lax.dot_general(lhs, rhs, (((0,), (0,)), ((), ())), preferred_element_type=F32)
            work[base + 8:, :] = work[base + 8:, :] - update[base + 8:, :]
    factor[...] = upper[...].T
    for cp in stores:
        cp.wait()


def per_device(sizes, fields):
    gy, gz, zc = sizes
    yc, xc = gy // CORES, gz // zc
    owners = xc * CORES
    vmem = pl.BlockSpec(memory_space=pltpu.VMEM)
    anywhere = pl.BlockSpec(memory_space=pl.ANY)
    grid_rows = jax.ShapeDtypeStruct((RY, N, RZ), F32)
    dma = pltpu.SemaphoreType.DMA

    def body(*refs):
        main_kernel(sizes, *refs)

    def channel(squares, diags):
        rows = squares * (N // owners) + diags
        return [
            pltpu.VMEM((owners, rows, N), F32),
            pltpu.VMEM((owners - 1, rows, N), F32),
            pltpu.VMEM((rows, N), F32),
            pltpu.VMEM((yc - 1, rows, N), F32),
            pltpu.VMEM((rows, N), F32),
            pltpu.VMEM((zc - 1, rows, N), F32),
            dma((owners - 1,)),
            dma((owners - 1,)),
            dma((yc - 1,)),
            dma((yc - 1,)),
            dma((zc - 1,)),
            dma((zc - 1,)),
        ]

    e, s, cross = pl.pallas_call(
        body,
        out_shape=(grid_rows, grid_rows, jax.ShapeDtypeStruct((N, N), F32)),
        in_specs=[pl.BlockSpec(memory_space=pltpu.HBM)],
        out_specs=(vmem, vmem, vmem),
        scratch_shapes=[
            pltpu.VMEM((3, RY + 4, N + 16, RZ), F32),
            pltpu.VMEM((N, RZ), F32),
            pltpu.VMEM((N, RZ), F32),
            pltpu.VMEM((N, RZ), F32),
            pltpu.VMEM((N, RZ), F32),
            pltpu.VMEM((2, N, RZ), F32),
            pltpu.VMEM((3, RY, N, RZ), F32),
            pltpu.VMEM((RY, N, RZ), F32),
            pltpu.VMEM((RY, N, RZ), F32),
            pltpu.VMEM((5, 2 * N, RY * RZ), BF16),
            pltpu.VMEM((3, N, RY * RZ), BF16),
            pltpu.VMEM((2 * RZ, 2 * RZ), BF16),
            pltpu.VMEM((2, N, N), F32),
            pltpu.VMEM((N, N), F32),
            dma((RY,)),
            dma((6,)),
            dma((6,)),
            dma((owners - 1,)),
            dma((owners - 1,)),
            *channel(2, 3),
            *channel(1, 2),
        ],
        compiler_params=pltpu.CompilerParams(collective_id=0, has_side_effects=True, vmem_limit_bytes=48 << 20),
        name="stencil_gram",
    )(pltpu.with_memory_space_constraint(fields, pltpu.HBM))
    whole = jax.ShapeDtypeStruct((N, RY, RZ), F32)
    return pl.pallas_call(
        factor_kernel,
        out_shape=(whole, whole, jax.ShapeDtypeStruct((N, N), F32)),
        in_specs=[vmem, vmem, vmem],
        out_specs=(anywhere, anywhere, vmem),
        scratch_shapes=[
            pltpu.VMEM((N, N), F32),
            pltpu.VMEM((N, N), F32),
            dma((2, RY)),
        ],
        compiler_params=pltpu.CompilerParams(vmem_limit_bytes=16 << 20),
        name="factor",
    )(cross, e, s)


def solution(mesh):
    gy, gz = mesh.shape["gy"], mesh.shape["gz"]
    sizes = (gy, gz, 8 if gz % 8 == 0 else 2)

    def call(fields):
        return per_device(sizes, fields)

    return jax.shard_map(
        call,
        mesh=mesh,
        in_specs=(P(None, None, "gy", "gz"),),
        out_specs=(P(None, "gy", "gz"), P(None, "gy", "gz"), P()),
        check_vma=False,
    )
```

```python
import jax
import jax.numpy as jnp
from jax import lax
from jax.experimental import pallas as pl
from jax.experimental.pallas import tpu as pltpu
from jax.sharding import PartitionSpec as P

MESH = pl.DeviceIdType.MESH
CORES = 2
N = 128
RY = 16
RZ = 128
X0 = 6
XC = X0 + 2
XB = 16
PARTS = 2
F32 = jnp.float32
BF16 = jnp.bfloat16


def ring_order(count):
    return sorted(range(1, count), key=lambda k: -min(k, count - k))


def main_kernel(
    sizes,
    fields,
    enst,
    strn,
    cross_out,
    fld,
    packs,
    pack_r,
    pack_l,
    from_left,
    from_right,
    edges,
    dz_buf,
    dxw_buf,
    dyw_buf,
    halves,
    thirds,
    band,
    grams,
    comb,
    load_sem,
    halo_send,
    halo_recv,
    ag_send,
    ag_recv,
    *channels,
):
    gy, gz, zc = sizes
    yc, xc = gy // CORES, gz // zc
    owners = xc * CORES
    own_rows = N // owners
    cells = gy * RY * gz * RZ
    g, h = lax.axis_index("gy"), lax.axis_index("gz")
    y, c = g // CORES, lax.rem(g, CORES)
    x, z = h // zc, lax.rem(h, zc)

    rs_peers = []
    for dx in ring_order(xc) + [0]:
        for dc in range(CORES):
            if dx or dc:
                slot = dx * CORES + dc - 1
                px, pc = lax.rem(x + dx, xc), lax.rem(c + dc, CORES)
                rs_peers.append((slot, px * CORES + pc, (y * CORES + pc, px * zc + z)))
    ey_peers = [(k - 1, (lax.rem(y + k, yc) * CORES + c, h)) for k in ring_order(yc)]
    ez_peers = [(k - 1, (g, x * zc + lax.rem(z + k, zc))) for k in ring_order(zc)]
    me = x * CORES + c
    up, down = (lax.rem(g + 1, gy), h), (lax.rem(g + gy - 1, gy), h)
    right, left = (g, lax.rem(h + 1, gz)), (g, lax.rem(h + gz - 1, gz))

    def remote(src, dst, send, recv, to):
        return pltpu.make_async_remote_copy(
            src_ref=src, dst_ref=dst, send_sem=send, recv_sem=recv, device_id=to, device_id_type=MESH
        )

    def load(row):
        return pltpu.make_async_copy(fields.at[:, :, row, :], fld.at[:, row + 2, pl.ds(X0, N + 4), :], load_sem.at[row])

    faces = (0, 1, RY - 2, RY - 1)
    for row in faces + tuple(range(2, RY - 2)):
        load(row).start()

    barrier = pltpu.get_barrier_semaphore()
    peers = [p for _, p in ey_peers + ez_peers] + [p for _, _, p in rs_peers] + [up, down, right, left]
    for p in peers:
        pl.semaphore_signal(barrier, inc=1, device_id=p, device_id_type=MESH)
    packs[...] = jnp.zeros_like(packs)
    for row in faces:
        load(row).wait()
    pl.semaphore_wait(barrier, len(peers))

    window = pl.ds(XC, N)

    def y_copy(way, r):
        slot = way * 2 + r
        src, dst = 2 + r + (RY - 2) * (1 - way), r + (RY + 2) * way
        to = (lax.rem(g + 1 + (gy - 2) * way, gy), h)
        return remote(
            fld.at[:, src, window, :], fld.at[:, dst, window, :], halo_send.at[slot], halo_recv.at[slot], to
        )

    sends = [y_copy(way, r) for way in range(2) for r in range(2)]
    for cp in sends:
        cp.start()

    def three_way(value):
        high = value.astype(BF16)
        rest = value - high.astype(F32)
        middle = rest.astype(BF16)
        return high, middle, (rest - middle.astype(F32)).astype(BF16)

    lane = lax.broadcasted_iota(jnp.int32, (XB, RZ), 1)
    group = lane // 4
    member = lane % 4
    low_half = member < 2

    def split_fields(row):
        cols = pl.ds(pl.multiple_of(row * RZ, RZ), RZ)
        places = [lax.rem(f * RY + row, 32) for f in range(3)]
        for b in range(N // XB):
            here = pl.ds(b * XB, XB)
            faces_here = []
            for f in range(3):
                value = fld[f, row + 2, pl.ds(XC + b * XB, XB), :]
                faces_here.append(pltpu.roll(value, lax.rem(4 * places[f] + 2, RZ), 1))
                high, middle, low = three_way(value)
                halves[f, here, cols] = high
                halves[f, pl.ds(N + b * XB, XB), cols] = middle
                thirds[f, here, cols] = low
            first = jnp.where(group == places[0], faces_here[0], packs[0, here, :])
            packs[0, here, :] = jnp.where(group == places[1], faces_here[1], first)
            packs[1, here, :] = jnp.where(group == places[2], faces_here[2], packs[1, here, :])

    def split_face(i, carry):
        split_fields(i + (RY - 4) * (i // 2))
        return carry

    def split_rest(row, carry):
        load(row).wait()
        split_fields(row)
        return carry

    lax.fori_loop(0, 4, split_face, 0)
    lax.fori_loop(2, RY - 2, split_rest, 0)

    for b in range(N // XB):
        here = pl.ds(b * XB, XB)
        lo, hi = packs[0, here, :], packs[1, here, :]
        pack_r[here, :] = jnp.where(low_half, lo, pltpu.roll(hi, 2, 1))
        pack_l[here, :] = jnp.where(low_half, pltpu.roll(lo, RZ - 2, 1), hi)
    z_halo = [
        remote(pack_r, from_left, halo_send.at[4], halo_recv.at[4], right),
        remote(pack_l, from_right, halo_send.at[5], halo_recv.at[5], left),
    ]
    for cp in z_halo:
        cp.start()
    sends += z_halo

    eye = lax.broadcasted_iota(jnp.int32, (N, N), 0) == lax.broadcasted_iota(jnp.int32, (N, N), 1)
    below = lax.broadcasted_iota(jnp.int32, (N, N), 0) > lax.broadcasted_iota(jnp.int32, (N, N), 1)

    def gram(q, cols):
        both = halves[q, :, cols]
        full = lax.dot_general(both, both, (((1,), (1,)), ((), ())), preferred_element_type=F32)
        return full[:N, :N] + full[:N, N:] + full[N:, :N] + full[N:, N:]

    def diagonal(m):
        return jnp.sum(jnp.where(eye, m, 0.0), axis=0, keepdims=True)

    def fill(piece, squares, diags):
        tail = jnp.concatenate(diags, axis=0)
        for o in range(owners):
            for k, value in enumerate(squares):
                piece[o, k * own_rows:(k + 1) * own_rows, :] = value[o * own_rows:(o + 1) * own_rows, :]
            piece[o, len(squares) * own_rows:, :] = tail

    class Channel:
        def __init__(self, piece, recv_a, sum_a, recv_b, sum_b, recv_c, rs_s, rs_r, ey_s, ey_r, ez_s, ez_r):
            self.piece, self.recv_a, self.sum_a = piece, recv_a, sum_a
            self.recv_b, self.sum_b, self.recv_c = recv_b, sum_b, recv_c
            self.rs = [remote(piece.at[o], recv_a.at[k], rs_s.at[k], rs_r.at[k], to) for k, o, to in rs_peers]
            self.ey = [remote(sum_a, recv_b.at[k], ey_s.at[k], ey_r.at[k], to) for k, to in ey_peers]
            self.ez = [remote(sum_b, recv_c.at[k], ez_s.at[k], ez_r.at[k], to) for k, to in ez_peers]

        def start(self, copies):
            for cp in copies:
                cp.start()

        def collect(self, copies, recv, own):
            for cp in copies:
                cp.wait_recv()
            for k in range(recv.shape[0]):
                own = own + recv[k]
            return own

        def scatter(self):
            self.start(self.rs)

        def along_y(self):
            self.sum_a[...] = self.collect(self.rs, self.recv_a, self.piece[me])
            self.start(self.ey)

        def along_z(self):
            self.sum_b[...] = self.collect(self.ey, self.recv_b, self.sum_a[...])
            self.start(self.ez)

        def total(self):
            return self.collect(self.ez, self.recv_c, self.sum_b[...])

    early, late = Channel(*channels[:12]), Channel(*channels[12:])
    everything = pl.ds(0, RY * RZ)
    gu, gv, gw = (gram(f, everything) for f in range(3))
    fill(early.piece, [jnp.where(below, gu, gv), gw], [diagonal(m) for m in (gu, gv, gw)])
    early.scatter()

    wide = 2 * RZ
    step = lax.broadcasted_iota(jnp.int32, (RZ, RZ), 1) - lax.broadcasted_iota(jnp.int32, (RZ, RZ), 0)
    weights = jnp.where(step == 2, 1.0, jnp.where(step == -2, -1.0, 0.0))
    weights = jnp.where(step == -1, 8.0, jnp.where(step == 1, -8.0, weights)).astype(BF16)
    band[...] = jnp.zeros_like(band)
    band[:RZ, :RZ] = weights
    band[RZ:, RZ:] = weights

    def inner_z(pair, part):
        rows = N // PARTS
        cols = pl.ds(pl.multiple_of(pair * wide, wide), wide)
        at = part * rows
        parts = [
            ref[f, pl.ds(first + at, rows), cols]
            for ref, first in ((halves, 0), (halves, N), (thirds, 0))
            for f in range(3)
        ]
        out = lax.dot_general(
            jnp.concatenate(parts, axis=0), band[...], (((1,), (0,)), ((), ())), preferred_element_type=F32
        )
        for f in range(3):
            for r in range(2):
                a, b, c2 = (out[(3 * k + f) * rows:(3 * k + f + 1) * rows, r * RZ:(r + 1) * RZ] for k in range(3))
                dz_buf[f, 2 * pair + r, pl.ds(at, rows), :] = a + b + c2

    def derivative(m2, m1, p1, p2):
        return 8.0 * (p1 - m1) + (m2 - p2)

    def without_z(row, blocks=range(N // XB)):
        for b in blocks:
            at = XC + b * XB

            def dx(f):
                return derivative(*(fld[f, row + 2, pl.ds(at + k, XB), :] for k in (-2, -1, 1, 2)))

            def dy(f):
                return derivative(*(fld[f, row + 2 + k, pl.ds(at, XB), :] for k in (-2, -1, 1, 2)))

            here = pl.ds(b * XB, XB)
            dxu, dxv, dyu, dyv = dx(0), dx(1), dy(0), dy(1)
            rotation, shear = dxv - dyu, dxv + dyu
            enst[row, here, :] = rotation * rotation
            strn[row, here, :] = 2.0 * (dxu * dxu + dyv * dyv) + shear * shear
            dxw_buf[row, here, :] = dx(2)
            dyw_buf[row, here, :] = dy(2)

    outer = (lane < 2) | (lane >= RZ - 2)

    def with_z(row):
        cols = pl.ds(pl.multiple_of(row * RZ, RZ), RZ)
        for b in range(N // XB):
            here = pl.ds(b * XB, XB)

            def dz(f):
                shift = lax.rem(RZ + RZ - 2 - 4 * lax.rem(f * RY + row, 32), RZ)
                edge = pltpu.roll(edges[0 if f < 2 else 1, here, :], shift, 1)
                return dz_buf[f, row, here, :] + jnp.where(outer, edge, 0.0)

            dzu, dzv, dzw = dz(0), dz(1), dz(2)
            dxw, dyw = dxw_buf[row, here, :], dyw_buf[row, here, :]
            r1, r2, s1, s2 = dxw - dzu, dyw - dzv, dxw + dzu, dyw + dzv
            e = (enst[row, here, :] + r1 * r1 + r2 * r2) * (1.0 / 288.0)
            s = (strn[row, here, :] + 2.0 * dzw * dzw + s1 * s1 + s2 * s2) * (1.0 / 288.0)
            enst[row, here, :] = e
            strn[row, here, :] = s
            for q, value in ((3, e), (4, s)):
                high = value.astype(BF16)
                halves[q, here, cols] = high
                halves[q, pl.ds(N + b * XB, XB), cols] = (value - high.astype(F32)).astype(BF16)

    def inner_pair(pair, carry):
        each = N // XB // PARTS
        for part in range(PARTS):
            inner_z(pair, part)
            for r in range(2):
                without_z(2 * pair + r, range(part * each, (part + 1) * each))
        return carry

    def face_pair(i, carry):
        for part in range(PARTS):
            inner_z(i * (RY // 2 - 1), part)
        return carry

    lax.fori_loop(1, RY // 2 - 1, inner_pair, 0)
    lax.fori_loop(0, 2, face_pair, 0)
    for cp in z_halo:
        cp.wait_recv()

    def edge(b, carry):
        here = pl.ds(pl.multiple_of(b * XB, XB), XB)
        lo, hi = from_left[here, :], from_right[here, :]
        joined = (
            jnp.where(low_half, lo, pltpu.roll(hi, 2, 1)),
            jnp.where(low_half, pltpu.roll(lo, RZ - 2, 1), hi),
        )
        for k, m in enumerate(joined):
            next2, next1 = pltpu.roll(m, RZ - 2, 1), pltpu.roll(m, RZ - 1, 1)
            last1, last2 = pltpu.roll(m, 1, 1), pltpu.roll(m, 2, 1)
            tops = jnp.where(member == 0, -next2, 8.0 * next1 - next2)
            bottoms = jnp.where(member == 2, last2 - 8.0 * last1, last2)
            edges[k, here, :] = jnp.where(low_half, tops, bottoms)
        return carry

    lax.fori_loop(0, N // XB, edge, 0)

    def inner_rows(pair, carry):
        with_z(2 * pair)
        with_z(2 * pair + 1)
        return carry

    lax.fori_loop(1, RY // 2 - 1, inner_rows, 0)
    inside = pl.ds(2 * RZ, (RY - 4) * RZ)
    for q in range(2):
        grams[q] = gram(3 + q, inside)

    def face(which):
        first = (RY - 2) * which
        for r in range(2):
            y_copy(which, r).wait_recv()

        def face_row(r, carry):
            without_z(first + r)
            with_z(first + r)
            return carry

        lax.fori_loop(0, 2, face_row, 0)
        cols = pl.ds(pl.multiple_of(first * RZ, wide), wide)
        for q in range(2):
            grams[q] = grams[q] + gram(3 + q, cols)

    face(lax.rem(1 + c, CORES))
    early.along_y()
    face(c)

    ge, gs = grams[0], grams[1]
    fill(late.piece, [jnp.where(below, ge, gs)], [diagonal(ge), diagonal(gs)])
    late.scatter()
    late.along_y()
    early.along_z()
    late.along_z()
    first_sums = early.total()
    last_sums = late.total()

    diag = jnp.concatenate([first_sums[2 * own_rows:, :], last_sums[own_rows:, :]], axis=0)
    trace = jnp.sum(diag, axis=1, keepdims=True)
    weight = 1.0 / (5.0 * cells * (trace / (N * cells) + 1e-6))
    wide_weights = [jnp.broadcast_to(weight[q:q + 1, :], (own_rows, N)) for q in range(5)]
    row_id = me * own_rows + lax.broadcasted_iota(jnp.int32, (own_rows, N), 0)
    lower = row_id > lax.broadcasted_iota(jnp.int32, (own_rows, N), 1)
    mine = pl.ds(pl.multiple_of(me * own_rows, own_rows), own_rows)
    comb[mine, :] = (
        first_sums[:own_rows, :] * jnp.where(lower, wide_weights[0], wide_weights[1])
        + first_sums[own_rows:2 * own_rows, :] * jnp.where(lower, wide_weights[2], 0.0)
        + last_sums[:own_rows, :] * jnp.where(lower, wide_weights[3], wide_weights[4])
    )
    ag = [remote(comb.at[mine, :], comb.at[mine, :], ag_send.at[k], ag_recv.at[k], to) for k, _, to in rs_peers]
    for cp in ag:
        cp.start()
    for cp in sends + early.rs + early.ey + early.ez + late.rs + late.ey + late.ez:
        cp.wait_send()
    middle = jnp.sum(diag * weight, axis=0, keepdims=True)
    for cp in ag:
        cp.wait_recv()
    square = jnp.where(eye, 0.0, comb[...])
    cross_out[...] = square + square.T + jnp.where(eye, jnp.broadcast_to(middle, (N, N)), 0.0)
    for cp in ag:
        cp.wait_send()


def factor_kernel(cross, e_in, s_in, e_out, s_out, factor, upper, spread, out_sem):
    stores = [
        pltpu.make_async_copy(src.at[r], dst.at[:, r, :], out_sem.at[q, r])
        for q, (src, dst) in enumerate(((e_in, e_out), (s_in, s_out)))
        for r in range(RY)
    ]
    for cp in stores:
        cp.start()
    lane = lax.broadcasted_iota(jnp.int32, (8, N), 1)
    sub = lax.broadcasted_iota(jnp.int32, (8, N), 0)
    count = N // 8
    blocks = [cross[8 * i:8 * i + 8, :] for i in range(count)]
    for p in range(count):
        base = 8 * p
        v = blocks[p]
        rows = [jnp.broadcast_to(v[k:k + 1, :], (8, N)) for k in range(8)]
        for m in range(8):
            spread[m] = jnp.broadcast_to(v[:, base + m:base + m + 1], (8, N))
        s = {(k, m): spread[m, pl.ds(k, 8, stride=0), :] for m in range(8) for k in range(m + 1)}
        columns = {
            (i, k): jnp.broadcast_to(blocks[i][:, base + k:base + k + 1], (8, N))
            for i in range(p + 1, count)
            for k in range(8)
        }
        inverse, u, panel = [], {}, None
        for k in range(8):
            inverse.append(lax.rsqrt(s[k, k]))
            for m in range(k + 1, 8):
                u[k, m] = s[k, m] * inverse[k]
            for m in range(k + 1, 8):
                for q in range(m, 8):
                    s[m, q] = s[m, q] - u[k, m] * u[k, q]
            rows[k] = rows[k] * inverse[k]
            for m in range(k + 1, 8):
                rows[m] = rows[m] - u[k, m] * rows[k]
            panel = rows[k] if panel is None else jnp.where(sub == k, rows[k], panel)
        upper[base:base + 8, :] = jnp.where(lane >= sub + base, panel, 0.0)
        if p == count - 1:
            break
        for k in range(7, -1, -1):
            rows[k] = rows[k] * inverse[k]
            for m in range(k):
                rows[m] = rows[m] - u[m, k] * rows[k]
        for i in range(p + 1, count):
            terms = [columns[i, k] * rows[k] for k in range(8)]
            while len(terms) > 1:
                terms = [terms[t] + terms[t + 1] for t in range(0, len(terms), 2)]
            blocks[i] = blocks[i] - terms[0]
    factor[...] = upper[...].T
    for cp in stores:
        cp.wait()


def per_device(sizes, fields):
    gy, gz, zc = sizes
    yc, xc = gy // CORES, gz // zc
    owners = xc * CORES
    vmem = pl.BlockSpec(memory_space=pltpu.VMEM)
    anywhere = pl.BlockSpec(memory_space=pl.ANY)
    grid_rows = jax.ShapeDtypeStruct((RY, N, RZ), F32)
    dma = pltpu.SemaphoreType.DMA

    def body(*refs):
        main_kernel(sizes, *refs)

    def channel(squares, diags):
        rows = squares * (N // owners) + diags
        return [
            pltpu.VMEM((owners, rows, N), F32),
            pltpu.VMEM((owners - 1, rows, N), F32),
            pltpu.VMEM((rows, N), F32),
            pltpu.VMEM((yc - 1, rows, N), F32),
            pltpu.VMEM((rows, N), F32),
            pltpu.VMEM((zc - 1, rows, N), F32),
            dma((owners - 1,)),
            dma((owners - 1,)),
            dma((yc - 1,)),
            dma((yc - 1,)),
            dma((zc - 1,)),
            dma((zc - 1,)),
        ]

    e, s, cross = pl.pallas_call(
        body,
        out_shape=(grid_rows, grid_rows, jax.ShapeDtypeStruct((N, N), F32)),
        in_specs=[pl.BlockSpec(memory_space=pltpu.HBM)],
        out_specs=(vmem, vmem, vmem),
        scratch_shapes=[
            pltpu.VMEM((3, RY + 4, N + 16, RZ), F32),
            pltpu.VMEM((2, N, RZ), F32),
            pltpu.VMEM((N, RZ), F32),
            pltpu.VMEM((N, RZ), F32),
            pltpu.VMEM((N, RZ), F32),
            pltpu.VMEM((N, RZ), F32),
            pltpu.VMEM((2, N, RZ), F32),
            pltpu.VMEM((3, RY, N, RZ), F32),
            pltpu.VMEM((RY, N, RZ), F32),
            pltpu.VMEM((RY, N, RZ), F32),
            pltpu.VMEM((5, 2 * N, RY * RZ), BF16),
            pltpu.VMEM((3, N, RY * RZ), BF16),
            pltpu.VMEM((2 * RZ, 2 * RZ), BF16),
            pltpu.VMEM((2, N, N), F32),
            pltpu.VMEM((N, N), F32),
            dma((RY,)),
            dma((6,)),
            dma((6,)),
            dma((owners - 1,)),
            dma((owners - 1,)),
            *channel(2, 3),
            *channel(1, 2),
        ],
        compiler_params=pltpu.CompilerParams(collective_id=0, has_side_effects=True, vmem_limit_bytes=48 << 20),
        name="stencil_gram",
    )(pltpu.with_memory_space_constraint(fields, pltpu.HBM))
    whole = jax.ShapeDtypeStruct((N, RY, RZ), F32)
    return pl.pallas_call(
        factor_kernel,
        out_shape=(whole, whole, jax.ShapeDtypeStruct((N, N), F32)),
        in_specs=[vmem, vmem, vmem],
        out_specs=(anywhere, anywhere, vmem),
        scratch_shapes=[
            pltpu.VMEM((N, N), F32),
            pltpu.VMEM((8, 8, N), F32),
            dma((2, RY)),
        ],
        compiler_params=pltpu.CompilerParams(vmem_limit_bytes=16 << 20),
        name="factor",
    )(cross, e, s)


def solution(mesh):
    gy, gz = mesh.shape["gy"], mesh.shape["gz"]
    sizes = (gy, gz, 8 if gz % 8 == 0 else 2)

    def call(fields):
        return per_device(sizes, fields)

    return jax.shard_map(
        call,
        mesh=mesh,
        in_specs=(P(None, None, "gy", "gz"),),
        out_specs=(P(None, "gy", "gz"), P(None, "gy", "gz"), P()),
        check_vma=False,
    )
```

```python
import jax
import jax.numpy as jnp
from jax import lax
from jax.experimental import pallas as pl
from jax.experimental.pallas import tpu as pltpu
from jax.sharding import PartitionSpec as P

MESH = pl.DeviceIdType.MESH
CORES = 2
N = 128
RY = 16
RZ = 128
X0 = 6
XC = X0 + 2
XB = 16
PARTS = 2
F32 = jnp.float32
BF16 = jnp.bfloat16


def ring_order(count):
    return sorted(range(1, count), key=lambda k: -min(k, count - k))


def main_kernel(
    sizes,
    fields,
    enst,
    strn,
    cross_out,
    fld,
    packs,
    pack_r,
    pack_l,
    from_left,
    from_right,
    edges,
    dz_buf,
    dxw_buf,
    dyw_buf,
    halves,
    thirds,
    band,
    comb,
    load_sem,
    halo_send,
    halo_recv,
    ag_send,
    ag_recv,
    *channels,
):
    gy, gz, zc = sizes
    yc, xc = gy // CORES, gz // zc
    owners = xc * CORES
    own_rows = N // owners
    cells = gy * RY * gz * RZ
    g, h = lax.axis_index("gy"), lax.axis_index("gz")
    y, c = g // CORES, lax.rem(g, CORES)
    x, z = h // zc, lax.rem(h, zc)

    rs_peers = []
    for dx in ring_order(xc) + [0]:
        for dc in range(CORES):
            if dx or dc:
                slot = dx * CORES + dc - 1
                px, pc = lax.rem(x + dx, xc), lax.rem(c + dc, CORES)
                rs_peers.append((slot, px * CORES + pc, (y * CORES + pc, px * zc + z)))
    ey_peers = [(k - 1, (lax.rem(y + k, yc) * CORES + c, h)) for k in ring_order(yc)]
    ez_peers = [(k - 1, (g, x * zc + lax.rem(z + k, zc))) for k in ring_order(zc)]
    me = x * CORES + c
    up, down = (lax.rem(g + 1, gy), h), (lax.rem(g + gy - 1, gy), h)
    right, left = (g, lax.rem(h + 1, gz)), (g, lax.rem(h + gz - 1, gz))

    def remote(src, dst, send, recv, to):
        return pltpu.make_async_remote_copy(
            src_ref=src, dst_ref=dst, send_sem=send, recv_sem=recv, device_id=to, device_id_type=MESH
        )

    def load(row):
        return pltpu.make_async_copy(fields.at[:, :, row, :], fld.at[:, row + 2, pl.ds(X0, N + 4), :], load_sem.at[row])

    faces = (0, 1, RY - 2, RY - 1)
    for row in faces + tuple(range(2, RY - 2)):
        load(row).start()

    barrier = pltpu.get_barrier_semaphore()
    peers = [p for _, p in ey_peers + ez_peers] + [p for _, _, p in rs_peers] + [up, down, right, left]
    for p in peers:
        pl.semaphore_signal(barrier, inc=1, device_id=p, device_id_type=MESH)
    packs[...] = jnp.zeros_like(packs)
    for row in faces:
        load(row).wait()
    pl.semaphore_wait(barrier, len(peers))

    window = pl.ds(XC, N)

    def y_copy(way, r):
        slot = way * 2 + r
        src, dst = 2 + r + (RY - 2) * (1 - way), r + (RY + 2) * way
        to = (lax.rem(g + 1 + (gy - 2) * way, gy), h)
        return remote(
            fld.at[:, src, window, :], fld.at[:, dst, window, :], halo_send.at[slot], halo_recv.at[slot], to
        )

    sends = [y_copy(way, r) for way in range(2) for r in range(2)]
    for cp in sends:
        cp.start()

    def three_way(value):
        high = value.astype(BF16)
        rest = value - high.astype(F32)
        middle = rest.astype(BF16)
        return high, middle, (rest - middle.astype(F32)).astype(BF16)

    lane = lax.broadcasted_iota(jnp.int32, (XB, RZ), 1)
    group = lane // 4
    member = lane % 4
    low_half = member < 2

    def split_fields(row):
        cols = pl.ds(pl.multiple_of(row * RZ, RZ), RZ)
        places = [lax.rem(f * RY + row, 32) for f in range(3)]
        for b in range(N // XB):
            here = pl.ds(b * XB, XB)
            faces_here = []
            for f in range(3):
                value = fld[f, row + 2, pl.ds(XC + b * XB, XB), :]
                faces_here.append(pltpu.roll(value, lax.rem(4 * places[f] + 2, RZ), 1))
                high, middle, low = three_way(value)
                halves[f, here, cols] = high
                halves[f, pl.ds(N + b * XB, XB), cols] = middle
                if f < 2:
                    thirds[f, here, cols] = low
            first = jnp.where(group == places[0], faces_here[0], packs[0, here, :])
            packs[0, here, :] = jnp.where(group == places[1], faces_here[1], first)
            packs[1, here, :] = jnp.where(group == places[2], faces_here[2], packs[1, here, :])

    def split_face(i, carry):
        split_fields(i + (RY - 4) * (i // 2))
        return carry

    def split_rest(row, carry):
        load(row).wait()
        split_fields(row)
        return carry

    lax.fori_loop(0, 4, split_face, 0)
    lax.fori_loop(2, RY - 2, split_rest, 0)

    for b in range(N // XB):
        here = pl.ds(b * XB, XB)
        lo, hi = packs[0, here, :], packs[1, here, :]
        pack_r[here, :] = jnp.where(low_half, lo, pltpu.roll(hi, 2, 1))
        pack_l[here, :] = jnp.where(low_half, pltpu.roll(lo, RZ - 2, 1), hi)
    z_halo = [
        remote(pack_r, from_left, halo_send.at[4], halo_recv.at[4], right),
        remote(pack_l, from_right, halo_send.at[5], halo_recv.at[5], left),
    ]
    for cp in z_halo:
        cp.start()
    sends += z_halo

    eye = lax.broadcasted_iota(jnp.int32, (N, N), 0) == lax.broadcasted_iota(jnp.int32, (N, N), 1)
    below = lax.broadcasted_iota(jnp.int32, (N, N), 0) > lax.broadcasted_iota(jnp.int32, (N, N), 1)

    def gram(q, cols):
        both = halves[q, :, cols]
        full = lax.dot_general(both, both, (((1,), (1,)), ((), ())), preferred_element_type=F32)
        return full[:N, :N] + full[:N, N:] + full[N:, :N] + full[N:, N:]

    def diagonal(m):
        return jnp.sum(jnp.where(eye, m, 0.0), axis=0, keepdims=True)

    def fill(piece, squares, diags):
        tail = jnp.concatenate(diags, axis=0)
        for o in range(owners):
            for k, value in enumerate(squares):
                piece[o, k * own_rows:(k + 1) * own_rows, :] = value[o * own_rows:(o + 1) * own_rows, :]
            piece[o, len(squares) * own_rows:, :] = tail

    class Channel:
        def __init__(self, piece, recv_a, sum_a, recv_b, sum_b, recv_c, rs_s, rs_r, ey_s, ey_r, ez_s, ez_r):
            self.piece, self.recv_a, self.sum_a = piece, recv_a, sum_a
            self.recv_b, self.sum_b, self.recv_c = recv_b, sum_b, recv_c
            self.rs = [remote(piece.at[o], recv_a.at[k], rs_s.at[k], rs_r.at[k], to) for k, o, to in rs_peers]
            self.ey = [remote(sum_a, recv_b.at[k], ey_s.at[k], ey_r.at[k], to) for k, to in ey_peers]
            self.ez = [remote(sum_b, recv_c.at[k], ez_s.at[k], ez_r.at[k], to) for k, to in ez_peers]

        def start(self, copies):
            for cp in copies:
                cp.start()

        def collect(self, copies, recv, own):
            for cp in copies:
                cp.wait_recv()
            for k in range(recv.shape[0]):
                own = own + recv[k]
            return own

        def scatter(self):
            self.start(self.rs)

        def along_y(self):
            self.sum_a[...] = self.collect(self.rs, self.recv_a, self.piece[me])
            self.start(self.ey)

        def along_z(self):
            self.sum_b[...] = self.collect(self.ey, self.recv_b, self.sum_a[...])
            self.start(self.ez)

        def total(self):
            return self.collect(self.ez, self.recv_c, self.sum_b[...])

    early, late = Channel(*channels[:12]), Channel(*channels[12:])
    everything = pl.ds(0, RY * RZ)
    gu, gv, gw = (gram(f, everything) for f in range(3))
    fill(early.piece, [jnp.where(below, gu, gv), gw], [diagonal(m) for m in (gu, gv, gw)])
    early.scatter()

    wide = 2 * RZ
    step = lax.broadcasted_iota(jnp.int32, (RZ, RZ), 1) - lax.broadcasted_iota(jnp.int32, (RZ, RZ), 0)
    weights = jnp.where(step == 2, 1.0, jnp.where(step == -2, -1.0, 0.0))
    weights = jnp.where(step == -1, 8.0, jnp.where(step == 1, -8.0, weights)).astype(BF16)
    band[...] = jnp.zeros_like(band)
    band[:RZ, :RZ] = weights
    band[RZ:, RZ:] = weights

    def inner_z(pair, part):
        rows = N // PARTS
        cols = pl.ds(pl.multiple_of(pair * wide, wide), wide)
        at = part * rows
        parts = [
            ref[f, pl.ds(first + at, rows), cols]
            for ref, first in ((halves, 0), (halves, N), (thirds, 0))
            for f in range(2)
        ]
        out = lax.dot_general(
            jnp.concatenate(parts, axis=0), band[...], (((1,), (0,)), ((), ())), preferred_element_type=F32
        )
        for f in range(2):
            for r in range(2):
                a, b, c2 = (out[(2 * k + f) * rows:(2 * k + f + 1) * rows, r * RZ:(r + 1) * RZ] for k in range(3))
                dz_buf[f, 2 * pair + r, pl.ds(at, rows), :] = a + b + c2

    def derivative(m2, m1, p1, p2):
        return 8.0 * (p1 - m1) + (m2 - p2)

    def wrapped_z(row, blocks):
        for b in blocks:
            w = fld[2, row + 2, pl.ds(XC + b * XB, XB), :]
            dz_buf[2, row, pl.ds(b * XB, XB), :] = derivative(*(pltpu.roll(w, k, 1) for k in (2, 1, RZ - 1, RZ - 2)))

    def without_z(row, blocks=range(N // XB)):
        for b in blocks:
            at = XC + b * XB

            def dx(f):
                return derivative(*(fld[f, row + 2, pl.ds(at + k, XB), :] for k in (-2, -1, 1, 2)))

            def dy(f):
                return derivative(*(fld[f, row + 2 + k, pl.ds(at, XB), :] for k in (-2, -1, 1, 2)))

            here = pl.ds(b * XB, XB)
            dxu, dxv, dyu, dyv = dx(0), dx(1), dy(0), dy(1)
            rotation, shear = dxv - dyu, dxv + dyu
            enst[row, here, :] = rotation * rotation
            strn[row, here, :] = 2.0 * (dxu * dxu + dyv * dyv) + shear * shear
            dxw_buf[row, here, :] = dx(2)
            dyw_buf[row, here, :] = dy(2)

    outer = (lane < 2) | (lane >= RZ - 2)

    def with_z(row):
        cols = pl.ds(row * RZ if isinstance(row, int) else pl.multiple_of(row * RZ, RZ), RZ)
        for b in range(N // XB):
            here = pl.ds(b * XB, XB)

            def dz(f):
                shift = (2 * RZ - 2 - 4 * ((f * RY + row) % 32)) % RZ
                edge = pltpu.roll(edges[0 if f < 2 else 1, here, :], shift, 1)
                return dz_buf[f, row, here, :] + jnp.where(outer, edge, 0.0)

            dzu, dzv, dzw = dz(0), dz(1), dz(2)
            dxw, dyw = dxw_buf[row, here, :], dyw_buf[row, here, :]
            r1, r2, s1, s2 = dxw - dzu, dyw - dzv, dxw + dzu, dyw + dzv
            e = (enst[row, here, :] + r1 * r1 + r2 * r2) * (1.0 / 288.0)
            s = (strn[row, here, :] + 2.0 * dzw * dzw + s1 * s1 + s2 * s2) * (1.0 / 288.0)
            enst[row, here, :] = e
            strn[row, here, :] = s
            for q, value in ((3, e), (4, s)):
                high = value.astype(BF16)
                halves[q, here, cols] = high
                halves[q, pl.ds(N + b * XB, XB), cols] = (value - high.astype(F32)).astype(BF16)

    def inner_pair(pair, carry):
        each = N // XB // PARTS
        for part in range(PARTS):
            inner_z(pair, part)
            for r in range(2):
                blocks = range(part * each, (part + 1) * each)
                wrapped_z(2 * pair + r, blocks)
                without_z(2 * pair + r, blocks)
        return carry

    def face_pair(i, carry):
        pair = i * (RY // 2 - 1)
        for part in range(PARTS):
            inner_z(pair, part)
        for r in range(2):
            wrapped_z(2 * pair + r, range(N // XB))
        return carry

    lax.fori_loop(1, RY // 2 - 1, inner_pair, 0)
    lax.fori_loop(0, 2, face_pair, 0)
    for cp in z_halo:
        cp.wait_recv()

    def edge(b, carry):
        here = pl.ds(pl.multiple_of(b * XB, XB), XB)
        lo, hi = from_left[here, :], from_right[here, :]
        joined = (
            jnp.where(low_half, lo, pltpu.roll(hi, 2, 1)),
            jnp.where(low_half, pltpu.roll(lo, RZ - 2, 1), hi),
        )
        for k, m in enumerate((joined[0], joined[1] - packs[1, here, :])):
            next2, next1 = pltpu.roll(m, RZ - 2, 1), pltpu.roll(m, RZ - 1, 1)
            last1, last2 = pltpu.roll(m, 1, 1), pltpu.roll(m, 2, 1)
            tops = jnp.where(member == 0, -next2, 8.0 * next1 - next2)
            bottoms = jnp.where(member == 2, last2 - 8.0 * last1, last2)
            edges[k, here, :] = jnp.where(low_half, tops, bottoms)
        return carry

    lax.fori_loop(0, N // XB, edge, 0)

    def inner_rows(pair, carry):
        with_z(2 * pair)
        with_z(2 * pair + 1)
        return carry

    lax.fori_loop(1, RY // 2 - 1, inner_rows, 0)
    for way in range(2):
        for r in range(2):
            y_copy(way, r).wait_recv()
    early.along_y()
    inside = [gram(3 + q, pl.ds(wide, (RY - 4) * RZ)) for q in range(2)]
    for row in faces:
        without_z(row)
        with_z(row)
    ge, gs = (
        inside[q] + gram(3 + q, pl.ds(0, wide)) + gram(3 + q, pl.ds((RY - 2) * RZ, wide)) for q in range(2)
    )

    fill(late.piece, [jnp.where(below, ge, gs)], [diagonal(ge), diagonal(gs)])
    late.scatter()
    late.along_y()
    early.along_z()
    late.along_z()
    first_sums = early.total()
    last_sums = late.total()

    diag = jnp.concatenate([first_sums[2 * own_rows:, :], last_sums[own_rows:, :]], axis=0)
    trace = jnp.sum(diag, axis=1, keepdims=True)
    weight = 1.0 / (5.0 * cells * (trace / (N * cells) + 1e-6))
    wide_weights = [jnp.broadcast_to(weight[q:q + 1, :], (own_rows, N)) for q in range(5)]
    row_id = me * own_rows + lax.broadcasted_iota(jnp.int32, (own_rows, N), 0)
    lower = row_id > lax.broadcasted_iota(jnp.int32, (own_rows, N), 1)
    mine = pl.ds(pl.multiple_of(me * own_rows, own_rows), own_rows)
    comb[mine, :] = (
        first_sums[:own_rows, :] * jnp.where(lower, wide_weights[0], wide_weights[1])
        + first_sums[own_rows:2 * own_rows, :] * jnp.where(lower, wide_weights[2], 0.0)
        + last_sums[:own_rows, :] * jnp.where(lower, wide_weights[3], wide_weights[4])
    )
    ag = [remote(comb.at[mine, :], comb.at[mine, :], ag_send.at[k], ag_recv.at[k], to) for k, _, to in rs_peers]
    for cp in ag:
        cp.start()
    for cp in sends + early.rs + early.ey + early.ez + late.rs + late.ey + late.ez:
        cp.wait_send()
    middle = jnp.sum(diag * weight, axis=0, keepdims=True)
    for cp in ag:
        cp.wait_recv()
    square = jnp.where(eye, 0.0, comb[...])
    cross_out[...] = square + square.T + jnp.where(eye, jnp.broadcast_to(middle, (N, N)), 0.0)
    for cp in ag:
        cp.wait_send()


def factor_kernel(cross, e_in, s_in, e_out, s_out, factor, upper, spread, out_sem):
    stores = [
        pltpu.make_async_copy(src.at[r], dst.at[:, r, :], out_sem.at[q, r])
        for q, (src, dst) in enumerate(((e_in, e_out), (s_in, s_out)))
        for r in range(RY)
    ]
    for cp in stores:
        cp.start()
    lane = lax.broadcasted_iota(jnp.int32, (8, N), 1)
    sub = lax.broadcasted_iota(jnp.int32, (8, N), 0)
    count = N // 8
    blocks = [cross[8 * i:8 * i + 8, :] for i in range(count)]
    for p in range(count):
        base = 8 * p
        v = blocks[p]
        rows = [jnp.broadcast_to(v[k:k + 1, :], (8, N)) for k in range(8)]
        for m in range(8):
            spread[m, 0:8, :] = jnp.broadcast_to(v[:, base + m:base + m + 1], (8, N))
        s = {(k, m): spread[m, pl.ds(k, 8, stride=0), :] for m in range(8) for k in range(m + 1)}
        columns = {
            (i, k): jnp.broadcast_to(blocks[i][:, base + k:base + k + 1], (8, N))
            for i in range(p + 1, count)
            for k in range(8)
        }
        inverse, u, panel = [], {}, None
        for k in range(8):
            inverse.append(lax.rsqrt(s[k, k]))
            for m in range(k + 1, 8):
                u[k, m] = s[k, m] * inverse[k]
            for m in range(k + 1, 8):
                for q in range(m, 8):
                    s[m, q] = s[m, q] - u[k, m] * u[k, q]
            rows[k] = rows[k] * inverse[k]
            for m in range(k + 1, 8):
                rows[m] = rows[m] - u[k, m] * rows[k]
            panel = rows[k] if panel is None else jnp.where(sub == k, rows[k], panel)
        upper[base:base + 8, :] = jnp.where(lane >= sub + base, panel, 0.0)
        if p == count - 1:
            break
        for k in range(7, -1, -1):
            rows[k] = rows[k] * inverse[k]
            for m in range(k):
                rows[m] = rows[m] - u[m, k] * rows[k]
        for i in range(p + 1, count):
            terms = [columns[i, k] * rows[k] for k in range(8)]
            while len(terms) > 1:
                terms = [terms[t] + terms[t + 1] for t in range(0, len(terms), 2)]
            blocks[i] = blocks[i] - terms[0]
    factor[...] = upper[...].T
    for cp in stores:
        cp.wait()


def per_device(sizes, fields):
    gy, gz, zc = sizes
    yc, xc = gy // CORES, gz // zc
    owners = xc * CORES
    vmem = pl.BlockSpec(memory_space=pltpu.VMEM)
    anywhere = pl.BlockSpec(memory_space=pl.ANY)
    grid_rows = jax.ShapeDtypeStruct((RY, N, RZ), F32)
    dma = pltpu.SemaphoreType.DMA

    def body(*refs):
        main_kernel(sizes, *refs)

    def channel(squares, diags):
        rows = squares * (N // owners) + diags
        return [
            pltpu.VMEM((owners, rows, N), F32),
            pltpu.VMEM((owners - 1, rows, N), F32),
            pltpu.VMEM((rows, N), F32),
            pltpu.VMEM((yc - 1, rows, N), F32),
            pltpu.VMEM((rows, N), F32),
            pltpu.VMEM((zc - 1, rows, N), F32),
            dma((owners - 1,)),
            dma((owners - 1,)),
            dma((yc - 1,)),
            dma((yc - 1,)),
            dma((zc - 1,)),
            dma((zc - 1,)),
        ]

    e, s, cross = pl.pallas_call(
        body,
        out_shape=(grid_rows, grid_rows, jax.ShapeDtypeStruct((N, N), F32)),
        in_specs=[pl.BlockSpec(memory_space=pltpu.HBM)],
        out_specs=(vmem, vmem, vmem),
        scratch_shapes=[
            pltpu.VMEM((3, RY + 4, N + 16, RZ), F32),
            pltpu.VMEM((2, N, RZ), F32),
            pltpu.VMEM((N, RZ), F32),
            pltpu.VMEM((N, RZ), F32),
            pltpu.VMEM((N, RZ), F32),
            pltpu.VMEM((N, RZ), F32),
            pltpu.VMEM((2, N, RZ), F32),
            pltpu.VMEM((3, RY, N, RZ), F32),
            pltpu.VMEM((RY, N, RZ), F32),
            pltpu.VMEM((RY, N, RZ), F32),
            pltpu.VMEM((5, 2 * N, RY * RZ), BF16),
            pltpu.VMEM((2, N, RY * RZ), BF16),
            pltpu.VMEM((2 * RZ, 2 * RZ), BF16),
            pltpu.VMEM((N, N), F32),
            dma((RY,)),
            dma((6,)),
            dma((6,)),
            dma((owners - 1,)),
            dma((owners - 1,)),
            *channel(2, 3),
            *channel(1, 2),
        ],
        compiler_params=pltpu.CompilerParams(collective_id=0, has_side_effects=True, vmem_limit_bytes=48 << 20),
        name="stencil_gram",
    )(pltpu.with_memory_space_constraint(fields, pltpu.HBM))
    whole = jax.ShapeDtypeStruct((N, RY, RZ), F32)
    return pl.pallas_call(
        factor_kernel,
        out_shape=(whole, whole, jax.ShapeDtypeStruct((N, N), F32)),
        in_specs=[vmem, vmem, vmem],
        out_specs=(anywhere, anywhere, vmem),
        scratch_shapes=[
            pltpu.VMEM((N, N), F32),
            pltpu.VMEM((8, 16, N), F32),
            dma((2, RY)),
        ],
        compiler_params=pltpu.CompilerParams(vmem_limit_bytes=16 << 20),
        name="factor",
    )(cross, e, s)


def solution(mesh):
    gy, gz = mesh.shape["gy"], mesh.shape["gz"]
    sizes = (gy, gz, 8 if gz % 8 == 0 else 2)

    def call(fields):
        return per_device(sizes, fields)

    return jax.shard_map(
        call,
        mesh=mesh,
        in_specs=(P(None, None, "gy", "gz"),),
        out_specs=(P(None, "gy", "gz"), P(None, "gy", "gz"), P()),
        check_vma=False,
    )
```

```python
import jax
import jax.numpy as jnp
from jax import lax
from jax.experimental import pallas as pl
from jax.experimental.pallas import tpu as pltpu
from jax.sharding import PartitionSpec as P

MESH = pl.DeviceIdType.MESH
CORES = 2
N = 128
RY = 16
RZ = 128
X0 = 6
XC = X0 + 2
XB = 16
PARTS = 2
F32 = jnp.float32
BF16 = jnp.bfloat16


def ring_order(count):
    return sorted(range(1, count), key=lambda k: -min(k, count - k))


def main_kernel(
    sizes,
    fields,
    enst,
    strn,
    cross_out,
    fld,
    packs,
    pack_r,
    pack_l,
    from_left,
    from_right,
    edges,
    dz_buf,
    dxw_buf,
    dyw_buf,
    halves,
    thirds,
    band,
    comb,
    load_sem,
    halo_send,
    halo_recv,
    ag_send,
    ag_recv,
    *channels,
):
    gy, gz, zc = sizes
    yc, xc = gy // CORES, gz // zc
    owners = xc * CORES
    own_rows = N // owners
    cells = gy * RY * gz * RZ
    g, h = lax.axis_index("gy"), lax.axis_index("gz")
    y, c = g // CORES, lax.rem(g, CORES)
    x, z = h // zc, lax.rem(h, zc)

    rs_peers = []
    for dx in ring_order(xc) + [0]:
        for dc in range(CORES):
            if dx or dc:
                slot = dx * CORES + dc - 1
                px, pc = lax.rem(x + dx, xc), lax.rem(c + dc, CORES)
                rs_peers.append((slot, px * CORES + pc, (y * CORES + pc, px * zc + z)))
    ey_peers = [(k - 1, (lax.rem(y + k, yc) * CORES + c, h)) for k in ring_order(yc)]
    ez_peers = [(k - 1, (g, x * zc + lax.rem(z + k, zc))) for k in ring_order(zc)]
    me = x * CORES + c
    up, down = (lax.rem(g + 1, gy), h), (lax.rem(g + gy - 1, gy), h)
    right, left = (g, lax.rem(h + 1, gz)), (g, lax.rem(h + gz - 1, gz))

    def remote(src, dst, send, recv, to):
        return pltpu.make_async_remote_copy(
            src_ref=src, dst_ref=dst, send_sem=send, recv_sem=recv, device_id=to, device_id_type=MESH
        )

    def load(row):
        return pltpu.make_async_copy(fields.at[:, :, row, :], fld.at[:, row + 2, pl.ds(X0, N + 4), :], load_sem.at[row])

    faces = (0, 1, RY - 2, RY - 1)
    for row in faces + tuple(range(2, RY - 2)):
        load(row).start()

    barrier = pltpu.get_barrier_semaphore()
    peers = [p for _, p in ey_peers + ez_peers] + [p for _, _, p in rs_peers] + [up, down, right, left]
    for p in peers:
        pl.semaphore_signal(barrier, inc=1, device_id=p, device_id_type=MESH)
    packs[...] = jnp.zeros_like(packs)
    for row in faces:
        load(row).wait()
    pl.semaphore_wait(barrier, len(peers))

    window = pl.ds(XC, N)

    def y_copy(way, r):
        slot = way * 2 + r
        src, dst = 2 + r + (RY - 2) * (1 - way), r + (RY + 2) * way
        to = (lax.rem(g + 1 + (gy - 2) * way, gy), h)
        return remote(
            fld.at[:, src, window, :], fld.at[:, dst, window, :], halo_send.at[slot], halo_recv.at[slot], to
        )

    sends = [y_copy(way, r) for way in range(2) for r in range(2)]
    for cp in sends:
        cp.start()

    def three_way(value):
        high = value.astype(BF16)
        rest = value - high.astype(F32)
        middle = rest.astype(BF16)
        return high, middle, (rest - middle.astype(F32)).astype(BF16)

    lane = lax.broadcasted_iota(jnp.int32, (XB, RZ), 1)
    narrow = lax.broadcasted_iota(jnp.int32, (8, RZ), 1) // 4
    member = lane % 4
    low_half = member < 2

    def split_fields(row):
        cols = pl.ds(pl.multiple_of(row * RZ, RZ), RZ)
        places = [lax.rem(f * RY + row, 32) for f in range(3)]
        for b in range(N // 8):
            here = pl.ds(b * 8, 8)
            faces_here = []
            for f in range(3):
                value = fld[f, row + 2, pl.ds(XC + b * 8, 8), :]
                faces_here.append(pltpu.roll(value, lax.rem(4 * places[f] + 2, RZ), 1))
                high, middle, low = three_way(value)
                halves[f, here, cols] = high
                halves[f, pl.ds(N + b * 8, 8), cols] = middle
                if f < 2:
                    thirds[f, here, cols] = low
            first = jnp.where(narrow == places[0], faces_here[0], packs[0, here, :])
            packs[0, here, :] = jnp.where(narrow == places[1], faces_here[1], first)
            packs[1, here, :] = jnp.where(narrow == places[2], faces_here[2], packs[1, here, :])

    wide = 2 * RZ
    step = lax.broadcasted_iota(jnp.int32, (RZ, RZ), 1) - lax.broadcasted_iota(jnp.int32, (RZ, RZ), 0)
    weights = jnp.where(step == 2, 1.0, jnp.where(step == -2, -1.0, 0.0))
    weights = jnp.where(step == -1, 8.0, jnp.where(step == 1, -8.0, weights)).astype(BF16)
    band[...] = jnp.zeros_like(band)
    band[:RZ, :RZ] = weights
    band[RZ:, RZ:] = weights

    def inner_z(pair, part):
        rows = N // PARTS
        cols = pl.ds(pl.multiple_of(pair * wide, wide), wide)
        at = part * rows
        parts = [
            ref[f, pl.ds(first + at, rows), cols]
            for ref, first in ((halves, 0), (halves, N), (thirds, 0))
            for f in range(2)
        ]
        out = lax.dot_general(
            jnp.concatenate(parts, axis=0), band[...], (((1,), (0,)), ((), ())), preferred_element_type=F32
        )
        for f in range(2):
            for r in range(2):
                a, b, c2 = (out[(2 * k + f) * rows:(2 * k + f + 1) * rows, r * RZ:(r + 1) * RZ] for k in range(3))
                dz_buf[f, 2 * pair + r, pl.ds(at, rows), :] = a + b + c2

    def split_face(i, carry):
        split_fields(i + (RY - 4) * (i // 2))
        return carry

    def split_rest(pair, carry):
        for r in range(2):
            load(2 * pair + r).wait()
        for part in range(PARTS):
            inner_z(pair - 1, part)
        for r in range(2):
            split_fields(2 * pair + r)
        return carry

    lax.fori_loop(0, 4, split_face, 0)
    lax.fori_loop(1, RY // 2 - 1, split_rest, 0)

    for b in range(N // XB):
        here = pl.ds(b * XB, XB)
        lo, hi = packs[0, here, :], packs[1, here, :]
        pack_r[here, :] = jnp.where(low_half, lo, pltpu.roll(hi, 2, 1))
        pack_l[here, :] = jnp.where(low_half, pltpu.roll(lo, RZ - 2, 1), hi)
    z_halo = [
        remote(pack_r, from_left, halo_send.at[4], halo_recv.at[4], right),
        remote(pack_l, from_right, halo_send.at[5], halo_recv.at[5], left),
    ]
    for cp in z_halo:
        cp.start()
    sends += z_halo

    eye = lax.broadcasted_iota(jnp.int32, (N, N), 0) == lax.broadcasted_iota(jnp.int32, (N, N), 1)
    below = lax.broadcasted_iota(jnp.int32, (N, N), 0) > lax.broadcasted_iota(jnp.int32, (N, N), 1)

    def gram(q, cols):
        both = halves[q, :, cols]
        full = lax.dot_general(both, both, (((1,), (1,)), ((), ())), preferred_element_type=F32)
        return full[:N, :N] + full[:N, N:] + full[N:, :N] + full[N:, N:]

    def diagonal(m):
        return jnp.sum(jnp.where(eye, m, 0.0), axis=0, keepdims=True)

    def fill(piece, squares, diags):
        tail = jnp.concatenate(diags, axis=0)
        for o in range(owners):
            for k, value in enumerate(squares):
                piece[o, k * own_rows:(k + 1) * own_rows, :] = value[o * own_rows:(o + 1) * own_rows, :]
            piece[o, len(squares) * own_rows:, :] = tail

    class Channel:
        def __init__(self, piece, recv_a, sum_a, recv_b, sum_b, recv_c, rs_s, rs_r, ey_s, ey_r, ez_s, ez_r):
            self.piece, self.recv_a, self.sum_a = piece, recv_a, sum_a
            self.recv_b, self.sum_b, self.recv_c = recv_b, sum_b, recv_c
            self.rs = [remote(piece.at[o], recv_a.at[k], rs_s.at[k], rs_r.at[k], to) for k, o, to in rs_peers]
            self.ey = [remote(sum_a, recv_b.at[k], ey_s.at[k], ey_r.at[k], to) for k, to in ey_peers]
            self.ez = [remote(sum_b, recv_c.at[k], ez_s.at[k], ez_r.at[k], to) for k, to in ez_peers]

        def start(self, copies):
            for cp in copies:
                cp.start()

        def collect(self, copies, recv, own):
            for cp in copies:
                cp.wait_recv()
            for k in range(recv.shape[0]):
                own = own + recv[k]
            return own

        def scatter(self):
            self.start(self.rs)

        def along_y(self):
            self.sum_a[...] = self.collect(self.rs, self.recv_a, self.piece[me])
            self.start(self.ey)

        def along_z(self):
            self.sum_b[...] = self.collect(self.ey, self.recv_b, self.sum_a[...])
            self.start(self.ez)

        def total(self):
            return self.collect(self.ez, self.recv_c, self.sum_b[...])

    early, late = Channel(*channels[:12]), Channel(*channels[12:])
    everything = pl.ds(0, RY * RZ)
    gu, gv, gw = (gram(f, everything) for f in range(3))
    fill(early.piece, [jnp.where(below, gu, gv), gw], [diagonal(m) for m in (gu, gv, gw)])
    early.scatter()

    def derivative(m2, m1, p1, p2):
        return 8.0 * (p1 - m1) + (m2 - p2)

    def wrapped_z(row, blocks):
        for b in blocks:
            w = fld[2, row + 2, pl.ds(XC + b * XB, XB), :]
            dz_buf[2, row, pl.ds(b * XB, XB), :] = derivative(*(pltpu.roll(w, k, 1) for k in (2, 1, RZ - 1, RZ - 2)))

    def without_z(row, blocks=range(N // XB)):
        for b in blocks:
            at = XC + b * XB

            def dx(f):
                return derivative(*(fld[f, row + 2, pl.ds(at + k, XB), :] for k in (-2, -1, 1, 2)))

            def dy(f):
                return derivative(*(fld[f, row + 2 + k, pl.ds(at, XB), :] for k in (-2, -1, 1, 2)))

            here = pl.ds(b * XB, XB)
            dxu, dxv, dyu, dyv = dx(0), dx(1), dy(0), dy(1)
            rotation, shear = dxv - dyu, dxv + dyu
            enst[row, here, :] = rotation * rotation
            strn[row, here, :] = 2.0 * (dxu * dxu + dyv * dyv) + shear * shear
            dxw_buf[row, here, :] = dx(2)
            dyw_buf[row, here, :] = dy(2)

    outer = (lane < 2) | (lane >= RZ - 2)

    def with_z(row):
        cols = pl.ds(row * RZ if isinstance(row, int) else pl.multiple_of(row * RZ, RZ), RZ)
        for b in range(N // XB):
            here = pl.ds(b * XB, XB)

            def dz(f):
                shift = (2 * RZ - 2 - 4 * ((f * RY + row) % 32)) % RZ
                edge = pltpu.roll(edges[0 if f < 2 else 1, here, :], shift, 1)
                return dz_buf[f, row, here, :] + jnp.where(outer, edge, 0.0)

            dzu, dzv, dzw = dz(0), dz(1), dz(2)
            dxw, dyw = dxw_buf[row, here, :], dyw_buf[row, here, :]
            r1, r2, s1, s2 = dxw - dzu, dyw - dzv, dxw + dzu, dyw + dzv
            e = (enst[row, here, :] + r1 * r1 + r2 * r2) * (1.0 / 288.0)
            s = (strn[row, here, :] + 2.0 * dzw * dzw + s1 * s1 + s2 * s2) * (1.0 / 288.0)
            enst[row, here, :] = e
            strn[row, here, :] = s
            for q, value in ((3, e), (4, s)):
                for t in range(XB // 8):
                    part = value[8 * t:8 * t + 8]
                    high = part.astype(BF16)
                    halves[q, pl.ds(b * XB + 8 * t, 8), cols] = high
                    halves[q, pl.ds(N + b * XB + 8 * t, 8), cols] = (part - high.astype(F32)).astype(BF16)

    def inner_pair(pair, carry):
        each = N // XB // PARTS
        for part in range(PARTS):
            for r in range(2):
                blocks = range(part * each, (part + 1) * each)
                wrapped_z(2 * pair + r, blocks)
                without_z(2 * pair + r, blocks)
        return carry

    def face_pair(i, carry):
        for part in range(PARTS):
            inner_z(RY // 2 - 2 + i, part)
        for r in range(2):
            wrapped_z((RY - 2) * i + r, range(N // XB))
        return carry

    lax.fori_loop(1, RY // 2 - 1, inner_pair, 0)
    lax.fori_loop(0, 2, face_pair, 0)
    for cp in z_halo:
        cp.wait_recv()

    def edge(b, carry):
        here = pl.ds(pl.multiple_of(b * XB, XB), XB)
        lo, hi = from_left[here, :], from_right[here, :]
        joined = (
            jnp.where(low_half, lo, pltpu.roll(hi, 2, 1)),
            jnp.where(low_half, pltpu.roll(lo, RZ - 2, 1), hi),
        )
        for k, m in enumerate((joined[0], joined[1] - packs[1, here, :])):
            next2, next1 = pltpu.roll(m, RZ - 2, 1), pltpu.roll(m, RZ - 1, 1)
            last1, last2 = pltpu.roll(m, 1, 1), pltpu.roll(m, 2, 1)
            tops = jnp.where(member == 0, -next2, 8.0 * next1 - next2)
            bottoms = jnp.where(member == 2, last2 - 8.0 * last1, last2)
            edges[k, here, :] = jnp.where(low_half, tops, bottoms)
        return carry

    lax.fori_loop(0, N // XB, edge, 0)

    def inner_rows(pair, carry):
        with_z(2 * pair)
        with_z(2 * pair + 1)
        return carry

    lax.fori_loop(1, RY // 2 - 1, inner_rows, 0)
    for way in range(2):
        for r in range(2):
            y_copy(way, r).wait_recv()
    early.along_y()
    inside = [gram(3 + q, pl.ds(wide, (RY - 4) * RZ)) for q in range(2)]
    for row in faces:
        without_z(row)
        with_z(row)
    ge, gs = (
        inside[q] + gram(3 + q, pl.ds(0, wide)) + gram(3 + q, pl.ds((RY - 2) * RZ, wide)) for q in range(2)
    )

    fill(late.piece, [jnp.where(below, ge, gs)], [diagonal(ge), diagonal(gs)])
    late.scatter()
    late.along_y()
    early.along_z()
    late.along_z()
    first_sums = early.total()
    last_sums = late.total()

    diag = jnp.concatenate([first_sums[2 * own_rows:, :], last_sums[own_rows:, :]], axis=0)
    trace = jnp.sum(diag, axis=1, keepdims=True)
    weight = 1.0 / (5.0 * cells * (trace / (N * cells) + 1e-6))
    wide_weights = [jnp.broadcast_to(weight[q:q + 1, :], (own_rows, N)) for q in range(5)]
    row_id = me * own_rows + lax.broadcasted_iota(jnp.int32, (own_rows, N), 0)
    lower = row_id > lax.broadcasted_iota(jnp.int32, (own_rows, N), 1)
    mine = pl.ds(pl.multiple_of(me * own_rows, own_rows), own_rows)
    comb[mine, :] = (
        first_sums[:own_rows, :] * jnp.where(lower, wide_weights[0], wide_weights[1])
        + first_sums[own_rows:2 * own_rows, :] * jnp.where(lower, wide_weights[2], 0.0)
        + last_sums[:own_rows, :] * jnp.where(lower, wide_weights[3], wide_weights[4])
    )
    ag = [remote(comb.at[mine, :], comb.at[mine, :], ag_send.at[k], ag_recv.at[k], to) for k, _, to in rs_peers]
    for cp in ag:
        cp.start()
    for cp in sends + early.rs + early.ey + early.ez + late.rs + late.ey + late.ez:
        cp.wait_send()
    middle = jnp.sum(diag * weight, axis=0, keepdims=True)
    for cp in ag:
        cp.wait_recv()
    square = jnp.where(eye, 0.0, comb[...])
    cross_out[...] = square + square.T + jnp.where(eye, jnp.broadcast_to(middle, (N, N)), 0.0)
    for cp in ag:
        cp.wait_send()


def factor_kernel(cross, e_in, s_in, e_out, s_out, factor, upper, spread, out_sem):
    stores = [
        pltpu.make_async_copy(src.at[r], dst.at[:, r, :], out_sem.at[q, r])
        for q, (src, dst) in enumerate(((e_in, e_out), (s_in, s_out)))
        for r in range(RY)
    ]
    lane = lax.broadcasted_iota(jnp.int32, (8, N), 1)
    sub = lax.broadcasted_iota(jnp.int32, (8, N), 0)
    count = N // 8
    blocks = [cross[8 * i:8 * i + 8, :] for i in range(count)]
    for p in range(count):
        base = 8 * p
        v = blocks[p]
        rows = [jnp.broadcast_to(v[k:k + 1, :], (8, N)) for k in range(8)]
        for m in range(8):
            spread[m, 0:8, :] = jnp.broadcast_to(v[:, base + m:base + m + 1], (8, N))
        s = {(k, m): spread[m, pl.ds(k, 8, stride=0), :] for m in range(8) for k in range(m + 1)}
        columns = {
            (i, k): jnp.broadcast_to(blocks[i][:, base + k:base + k + 1], (8, N))
            for i in range(p + 1, count)
            for k in range(8)
        }
        for cp in stores[4 * p:4 * p + 4]:
            cp.start()
        inverse, u, panel = [], {}, None
        for k in range(8):
            inverse.append(lax.rsqrt(s[k, k]))
            for m in range(k + 1, 8):
                u[k, m] = s[k, m] * inverse[k]
            for m in range(k + 1, 8):
                for q in range(m, 8):
                    s[m, q] = s[m, q] - u[k, m] * u[k, q]
            rows[k] = rows[k] * inverse[k]
            for m in range(k + 1, 8):
                rows[m] = rows[m] - u[k, m] * rows[k]
            panel = rows[k] if panel is None else jnp.where(sub == k, rows[k], panel)
        upper[base:base + 8, :] = jnp.where(lane >= sub + base, panel, 0.0)
        if p == count - 1:
            break
        for k in range(7, -1, -1):
            rows[k] = rows[k] * inverse[k]
            for m in range(k):
                rows[m] = rows[m] - u[m, k] * rows[k]
        for i in range(p + 1, count):
            terms = [columns[i, k] * rows[k] for k in range(8)]
            while len(terms) > 1:
                terms = [terms[t] + terms[t + 1] for t in range(0, len(terms), 2)]
            blocks[i] = blocks[i] - terms[0]
    factor[...] = upper[...].T
    for cp in stores:
        cp.wait()


def per_device(sizes, fields):
    gy, gz, zc = sizes
    yc, xc = gy // CORES, gz // zc
    owners = xc * CORES
    vmem = pl.BlockSpec(memory_space=pltpu.VMEM)
    anywhere = pl.BlockSpec(memory_space=pl.ANY)
    grid_rows = jax.ShapeDtypeStruct((RY, N, RZ), F32)
    dma = pltpu.SemaphoreType.DMA

    def body(*refs):
        main_kernel(sizes, *refs)

    def channel(squares, diags):
        rows = squares * (N // owners) + diags
        return [
            pltpu.VMEM((owners, rows, N), F32),
            pltpu.VMEM((owners - 1, rows, N), F32),
            pltpu.VMEM((rows, N), F32),
            pltpu.VMEM((yc - 1, rows, N), F32),
            pltpu.VMEM((rows, N), F32),
            pltpu.VMEM((zc - 1, rows, N), F32),
            dma((owners - 1,)),
            dma((owners - 1,)),
            dma((yc - 1,)),
            dma((yc - 1,)),
            dma((zc - 1,)),
            dma((zc - 1,)),
        ]

    e, s, cross = pl.pallas_call(
        body,
        out_shape=(grid_rows, grid_rows, jax.ShapeDtypeStruct((N, N), F32)),
        in_specs=[pl.BlockSpec(memory_space=pltpu.HBM)],
        out_specs=(vmem, vmem, vmem),
        scratch_shapes=[
            pltpu.VMEM((3, RY + 4, N + 16, RZ), F32),
            pltpu.VMEM((2, N, RZ), F32),
            pltpu.VMEM((N, RZ), F32),
            pltpu.VMEM((N, RZ), F32),
            pltpu.VMEM((N, RZ), F32),
            pltpu.VMEM((N, RZ), F32),
            pltpu.VMEM((2, N, RZ), F32),
            pltpu.VMEM((3, RY, N, RZ), F32),
            pltpu.VMEM((RY, N, RZ), F32),
            pltpu.VMEM((RY, N, RZ), F32),
            pltpu.VMEM((5, 2 * N, RY * RZ), BF16),
            pltpu.VMEM((2, N, RY * RZ), BF16),
            pltpu.VMEM((2 * RZ, 2 * RZ), BF16),
            pltpu.VMEM((N, N), F32),
            dma((RY,)),
            dma((6,)),
            dma((6,)),
            dma((owners - 1,)),
            dma((owners - 1,)),
            *channel(2, 3),
            *channel(1, 2),
        ],
        compiler_params=pltpu.CompilerParams(collective_id=0, has_side_effects=True, vmem_limit_bytes=48 << 20),
        name="stencil_gram",
    )(pltpu.with_memory_space_constraint(fields, pltpu.HBM))
    whole = jax.ShapeDtypeStruct((N, RY, RZ), F32)
    return pl.pallas_call(
        factor_kernel,
        out_shape=(whole, whole, jax.ShapeDtypeStruct((N, N), F32)),
        in_specs=[vmem, vmem, vmem],
        out_specs=(anywhere, anywhere, vmem),
        scratch_shapes=[
            pltpu.VMEM((N, N), F32),
            pltpu.VMEM((8, 16, N), F32),
            dma((2, RY)),
        ],
        compiler_params=pltpu.CompilerParams(vmem_limit_bytes=16 << 20),
        name="factor",
    )(cross, e, s)


def solution(mesh):
    gy, gz = mesh.shape["gy"], mesh.shape["gz"]
    sizes = (gy, gz, 8 if gz % 8 == 0 else 2)

    def call(fields):
        return per_device(sizes, fields)

    return jax.shard_map(
        call,
        mesh=mesh,
        in_specs=(P(None, None, "gy", "gz"),),
        out_specs=(P(None, "gy", "gz"), P(None, "gy", "gz"), P()),
        check_vma=False,
    )
```

```python
import jax
import jax.numpy as jnp
from jax import lax
from jax.experimental import pallas as pl
from jax.experimental.pallas import tpu as pltpu
from jax.sharding import PartitionSpec as P

MESH = pl.DeviceIdType.MESH
CORES = 2
N = 128
RY = 16
RZ = 128
X0 = 6
XC = X0 + 2
XB = 16
PARTS = 2
F32 = jnp.float32
BF16 = jnp.bfloat16


def ring_order(count):
    return sorted(range(1, count), key=lambda k: -min(k, count - k))


def main_kernel(
    sizes,
    fields,
    enst,
    strn,
    cross_out,
    fld,
    packs,
    pack_r,
    pack_l,
    from_left,
    from_right,
    edges,
    dz_buf,
    dxw_buf,
    dyw_buf,
    halves,
    thirds,
    band,
    comb,
    load_sem,
    halo_send,
    halo_recv,
    ag_send,
    ag_recv,
    *channels,
):
    gy, gz, zc = sizes
    yc, xc = gy // CORES, gz // zc
    owners = xc * CORES
    own_rows = N // owners
    cells = gy * RY * gz * RZ
    g, h = lax.axis_index("gy"), lax.axis_index("gz")
    y, c = g // CORES, lax.rem(g, CORES)
    x, z = h // zc, lax.rem(h, zc)

    rs_peers = []
    for dx in ring_order(xc) + [0]:
        for dc in range(CORES):
            if dx or dc:
                slot = dx * CORES + dc - 1
                px, pc = lax.rem(x + dx, xc), lax.rem(c + dc, CORES)
                rs_peers.append((slot, px * CORES + pc, (y * CORES + pc, px * zc + z)))
    ey_peers = [(k - 1, (lax.rem(y + k, yc) * CORES + c, h)) for k in ring_order(yc)]
    ez_peers = [(k - 1, (g, x * zc + lax.rem(z + k, zc))) for k in ring_order(zc)]
    me = x * CORES + c
    up, down = (lax.rem(g + 1, gy), h), (lax.rem(g + gy - 1, gy), h)
    right, left = (g, lax.rem(h + 1, gz)), (g, lax.rem(h + gz - 1, gz))

    def remote(src, dst, send, recv, to):
        return pltpu.make_async_remote_copy(
            src_ref=src, dst_ref=dst, send_sem=send, recv_sem=recv, device_id=to, device_id_type=MESH
        )

    def load(row):
        return pltpu.make_async_copy(fields.at[:, :, row, :], fld.at[:, row + 2, pl.ds(X0, N + 4), :], load_sem.at[row])

    faces = (0, 1, RY - 2, RY - 1)
    for row in faces + tuple(range(2, RY - 2)):
        load(row).start()

    barrier = pltpu.get_barrier_semaphore()
    peers = [p for _, p in ey_peers + ez_peers] + [p for _, _, p in rs_peers] + [up, down, right, left]
    for p in peers:
        pl.semaphore_signal(barrier, inc=1, device_id=p, device_id_type=MESH)
    packs[...] = jnp.zeros_like(packs)
    for row in faces:
        load(row).wait()
    pl.semaphore_wait(barrier, len(peers))

    window = pl.ds(XC, N)

    def y_copy(way, r):
        slot = way * 2 + r
        src, dst = 2 + r + (RY - 2) * (1 - way), r + (RY + 2) * way
        to = (lax.rem(g + 1 + (gy - 2) * way, gy), h)
        return remote(
            fld.at[:, src, window, :], fld.at[:, dst, window, :], halo_send.at[slot], halo_recv.at[slot], to
        )

    sends = [y_copy(way, r) for way in range(2) for r in range(2)]
    for cp in sends:
        cp.start()

    def three_way(value):
        high = value.astype(BF16)
        rest = value - high.astype(F32)
        middle = rest.astype(BF16)
        return high, middle, (rest - middle.astype(F32)).astype(BF16)

    lane = lax.broadcasted_iota(jnp.int32, (XB, RZ), 1)
    narrow = lax.broadcasted_iota(jnp.int32, (8, RZ), 1) // 4
    member = lane % 4
    low_half = member < 2

    def split_fields(row):
        cols = pl.ds(pl.multiple_of(row * RZ, RZ), RZ)
        places = [lax.rem(f * RY + row, 32) for f in range(3)]
        for b in range(N // 8):
            here = pl.ds(b * 8, 8)
            faces_here = []
            for f in range(3):
                value = fld[f, row + 2, pl.ds(XC + b * 8, 8), :]
                faces_here.append(pltpu.roll(value, lax.rem(4 * places[f] + 2, RZ), 1))
                high, middle, low = three_way(value)
                halves[f, here, cols] = high
                halves[f, pl.ds(N + b * 8, 8), cols] = middle
                if f < 2:
                    thirds[f, here, cols] = low
            first = jnp.where(narrow == places[0], faces_here[0], packs[0, here, :])
            packs[0, here, :] = jnp.where(narrow == places[1], faces_here[1], first)
            packs[1, here, :] = jnp.where(narrow == places[2], faces_here[2], packs[1, here, :])

    def split_face(i, carry):
        split_fields(i + (RY - 4) * (i // 2))
        return carry

    def split_rest(row, carry):
        load(row).wait()
        split_fields(row)
        return carry

    lax.fori_loop(0, 4, split_face, 0)
    lax.fori_loop(2, RY - 2, split_rest, 0)

    for b in range(N // XB):
        here = pl.ds(b * XB, XB)
        lo, hi = packs[0, here, :], packs[1, here, :]
        pack_r[here, :] = jnp.where(low_half, lo, pltpu.roll(hi, 2, 1))
        pack_l[here, :] = jnp.where(low_half, pltpu.roll(lo, RZ - 2, 1), hi)
    z_halo = [
        remote(pack_r, from_left, halo_send.at[4], halo_recv.at[4], right),
        remote(pack_l, from_right, halo_send.at[5], halo_recv.at[5], left),
    ]
    for cp in z_halo:
        cp.start()
    sends += z_halo

    eye = lax.broadcasted_iota(jnp.int32, (N, N), 0) == lax.broadcasted_iota(jnp.int32, (N, N), 1)
    below = lax.broadcasted_iota(jnp.int32, (N, N), 0) > lax.broadcasted_iota(jnp.int32, (N, N), 1)

    def gram(q, cols):
        both = halves[q, :, cols]
        full = lax.dot_general(both, both, (((1,), (1,)), ((), ())), preferred_element_type=F32)
        return full[:N, :N] + full[:N, N:] + full[N:, :N] + full[N:, N:]

    def diagonal(m):
        return jnp.sum(jnp.where(eye, m, 0.0), axis=0, keepdims=True)

    def fill(piece, squares, diags):
        tail = jnp.concatenate(diags, axis=0)
        for o in range(owners):
            for k, value in enumerate(squares):
                piece[o, k * own_rows:(k + 1) * own_rows, :] = value[o * own_rows:(o + 1) * own_rows, :]
            piece[o, len(squares) * own_rows:, :] = tail

    class Channel:
        def __init__(self, piece, recv_a, sum_a, recv_b, sum_b, recv_c, rs_s, rs_r, ey_s, ey_r, ez_s, ez_r):
            self.piece, self.recv_a, self.sum_a = piece, recv_a, sum_a
            self.recv_b, self.sum_b, self.recv_c = recv_b, sum_b, recv_c
            self.rs = [remote(piece.at[o], recv_a.at[k], rs_s.at[k], rs_r.at[k], to) for k, o, to in rs_peers]
            self.ey = [remote(sum_a, recv_b.at[k], ey_s.at[k], ey_r.at[k], to) for k, to in ey_peers]
            self.ez = [remote(sum_b, recv_c.at[k], ez_s.at[k], ez_r.at[k], to) for k, to in ez_peers]

        def start(self, copies):
            for cp in copies:
                cp.start()

        def collect(self, copies, recv, own):
            for cp in copies:
                cp.wait_recv()
            for k in range(recv.shape[0]):
                own = own + recv[k]
            return own

        def scatter(self):
            self.start(self.rs)

        def along_y(self):
            self.sum_a[...] = self.collect(self.rs, self.recv_a, self.piece[me])
            self.start(self.ey)

        def along_z(self):
            self.sum_b[...] = self.collect(self.ey, self.recv_b, self.sum_a[...])
            self.start(self.ez)

        def total(self):
            return self.collect(self.ez, self.recv_c, self.sum_b[...])

    early, late = Channel(*channels[:12]), Channel(*channels[12:])
    everything = pl.ds(0, RY * RZ)
    gu, gv, gw = (gram(f, everything) for f in range(3))
    fill(early.piece, [jnp.where(below, gu, gv), gw], [diagonal(m) for m in (gu, gv, gw)])
    early.scatter()

    wide = 2 * RZ
    step = lax.broadcasted_iota(jnp.int32, (RZ, RZ), 1) - lax.broadcasted_iota(jnp.int32, (RZ, RZ), 0)
    weights = jnp.where(step == 2, 1.0, jnp.where(step == -2, -1.0, 0.0))
    weights = jnp.where(step == -1, 8.0, jnp.where(step == 1, -8.0, weights)).astype(BF16)
    band[...] = jnp.zeros_like(band)
    band[:RZ, :RZ] = weights
    band[RZ:, RZ:] = weights

    def inner_z(pair, part):
        rows = N // PARTS
        cols = pl.ds(pl.multiple_of(pair * wide, wide), wide)
        at = part * rows
        parts = [
            ref[f, pl.ds(first + at, rows), cols]
            for ref, first in ((halves, 0), (halves, N), (thirds, 0))
            for f in range(2)
        ]
        out = lax.dot_general(
            jnp.concatenate(parts, axis=0), band[...], (((1,), (0,)), ((), ())), preferred_element_type=F32
        )
        for f in range(2):
            for r in range(2):
                a, b, c2 = (out[(2 * k + f) * rows:(2 * k + f + 1) * rows, r * RZ:(r + 1) * RZ] for k in range(3))
                dz_buf[f, 2 * pair + r, pl.ds(at, rows), :] = a + b + c2

    def derivative(m2, m1, p1, p2):
        return 8.0 * (p1 - m1) + (m2 - p2)

    def wrapped_z(row, blocks):
        for b in blocks:
            w = fld[2, row + 2, pl.ds(XC + b * XB, XB), :]
            dz_buf[2, row, pl.ds(b * XB, XB), :] = derivative(*(pltpu.roll(w, k, 1) for k in (2, 1, RZ - 1, RZ - 2)))

    def without_z(row, blocks=range(N // XB)):
        for b in blocks:
            at = XC + b * XB

            def dx(f):
                return derivative(*(fld[f, row + 2, pl.ds(at + k, XB), :] for k in (-2, -1, 1, 2)))

            def dy(f):
                return derivative(*(fld[f, row + 2 + k, pl.ds(at, XB), :] for k in (-2, -1, 1, 2)))

            here = pl.ds(b * XB, XB)
            dxu, dxv, dyu, dyv = dx(0), dx(1), dy(0), dy(1)
            rotation, shear = dxv - dyu, dxv + dyu
            enst[row, here, :] = rotation * rotation
            strn[row, here, :] = 2.0 * (dxu * dxu + dyv * dyv) + shear * shear
            dxw_buf[row, here, :] = dx(2)
            dyw_buf[row, here, :] = dy(2)

    outer = (lane < 2) | (lane >= RZ - 2)

    def with_z(row):
        cols = pl.ds(row * RZ if isinstance(row, int) else pl.multiple_of(row * RZ, RZ), RZ)
        for b in range(N // XB):
            here = pl.ds(b * XB, XB)

            def dz(f):
                shift = (2 * RZ - 2 - 4 * ((f * RY + row) % 32)) % RZ
                edge = pltpu.roll(edges[0 if f < 2 else 1, here, :], shift, 1)
                return dz_buf[f, row, here, :] + jnp.where(outer, edge, 0.0)

            dzu, dzv, dzw = dz(0), dz(1), dz(2)
            dxw, dyw = dxw_buf[row, here, :], dyw_buf[row, here, :]
            r1, r2, s1, s2 = dxw - dzu, dyw - dzv, dxw + dzu, dyw + dzv
            e = (enst[row, here, :] + r1 * r1 + r2 * r2) * (1.0 / 288.0)
            s = (strn[row, here, :] + 2.0 * dzw * dzw + s1 * s1 + s2 * s2) * (1.0 / 288.0)
            enst[row, here, :] = e
            strn[row, here, :] = s
            for q, value in ((3, e), (4, s)):
                for t in range(XB // 8):
                    part = value[8 * t:8 * t + 8]
                    high = part.astype(BF16)
                    halves[q, pl.ds(b * XB + 8 * t, 8), cols] = high
                    halves[q, pl.ds(N + b * XB + 8 * t, 8), cols] = (part - high.astype(F32)).astype(BF16)

    def inner_pair(pair, carry):
        each = N // XB // PARTS
        for part in range(PARTS):
            inner_z(pair, part)
            for r in range(2):
                blocks = range(part * each, (part + 1) * each)
                wrapped_z(2 * pair + r, blocks)
                without_z(2 * pair + r, blocks)
        return carry

    def face_pair(i, carry):
        pair = i * (RY // 2 - 1)
        for part in range(PARTS):
            inner_z(pair, part)
        for r in range(2):
            wrapped_z(2 * pair + r, range(N // XB))
        return carry

    lax.fori_loop(1, RY // 2 - 1, inner_pair, 0)
    lax.fori_loop(0, 2, face_pair, 0)
    for way in range(2):
        for r in range(2):
            y_copy(way, r).wait_recv()

    def face_row(i, carry):
        without_z(i + (RY - 4) * (i // 2))
        return carry

    lax.fori_loop(0, 4, face_row, 0)
    for cp in z_halo:
        cp.wait_recv()

    def edge(b, carry):
        here = pl.ds(pl.multiple_of(b * XB, XB), XB)
        lo, hi = from_left[here, :], from_right[here, :]
        joined = (
            jnp.where(low_half, lo, pltpu.roll(hi, 2, 1)),
            jnp.where(low_half, pltpu.roll(lo, RZ - 2, 1), hi),
        )
        for k, m in enumerate((joined[0], joined[1] - packs[1, here, :])):
            next2, next1 = pltpu.roll(m, RZ - 2, 1), pltpu.roll(m, RZ - 1, 1)
            last1, last2 = pltpu.roll(m, 1, 1), pltpu.roll(m, 2, 1)
            tops = jnp.where(member == 0, -next2, 8.0 * next1 - next2)
            bottoms = jnp.where(member == 2, last2 - 8.0 * last1, last2)
            edges[k, here, :] = jnp.where(low_half, tops, bottoms)
        return carry

    lax.fori_loop(0, N // XB, edge, 0)

    def inner_rows(pair, carry):
        with_z(2 * pair)
        with_z(2 * pair + 1)
        return carry

    lax.fori_loop(1, RY // 2 - 1, inner_rows, 0)
    early.along_y()
    inside = [gram(3 + q, pl.ds(wide, (RY - 4) * RZ)) for q in range(2)]
    for row in faces:
        with_z(row)
    ge, gs = (
        inside[q] + gram(3 + q, pl.ds(0, wide)) + gram(3 + q, pl.ds((RY - 2) * RZ, wide)) for q in range(2)
    )

    fill(late.piece, [jnp.where(below, ge, gs)], [diagonal(ge), diagonal(gs)])
    late.scatter()
    late.along_y()
    early.along_z()
    late.along_z()
    first_sums = early.total()
    last_sums = late.total()

    diag = jnp.concatenate([first_sums[2 * own_rows:, :], last_sums[own_rows:, :]], axis=0)
    trace = jnp.sum(diag, axis=1, keepdims=True)
    weight = 1.0 / (5.0 * cells * (trace / (N * cells) + 1e-6))
    wide_weights = [jnp.broadcast_to(weight[q:q + 1, :], (own_rows, N)) for q in range(5)]
    row_id = me * own_rows + lax.broadcasted_iota(jnp.int32, (own_rows, N), 0)
    lower = row_id > lax.broadcasted_iota(jnp.int32, (own_rows, N), 1)
    mine = pl.ds(pl.multiple_of(me * own_rows, own_rows), own_rows)
    comb[mine, :] = (
        first_sums[:own_rows, :] * jnp.where(lower, wide_weights[0], wide_weights[1])
        + first_sums[own_rows:2 * own_rows, :] * jnp.where(lower, wide_weights[2], 0.0)
        + last_sums[:own_rows, :] * jnp.where(lower, wide_weights[3], wide_weights[4])
    )
    ag = [remote(comb.at[mine, :], comb.at[mine, :], ag_send.at[k], ag_recv.at[k], to) for k, _, to in rs_peers]
    for cp in ag:
        cp.start()
    for cp in sends + early.rs + early.ey + early.ez + late.rs + late.ey + late.ez:
        cp.wait_send()
    middle = jnp.sum(diag * weight, axis=0, keepdims=True)
    for cp in ag:
        cp.wait_recv()
    square = jnp.where(eye, 0.0, comb[...])
    cross_out[...] = square + square.T + jnp.where(eye, jnp.broadcast_to(middle, (N, N)), 0.0)
    for cp in ag:
        cp.wait_send()


def factor_kernel(cross, e_in, s_in, e_out, s_out, factor, upper, spread, out_sem):
    stores = [
        pltpu.make_async_copy(src.at[r], dst.at[:, r, :], out_sem.at[q, r])
        for q, (src, dst) in enumerate(((e_in, e_out), (s_in, s_out)))
        for r in range(RY)
    ]
    lane = lax.broadcasted_iota(jnp.int32, (8, N), 1)
    sub = lax.broadcasted_iota(jnp.int32, (8, N), 0)
    count = N // 8
    blocks = [cross[8 * i:8 * i + 8, :] for i in range(count)]
    for p in range(count):
        base = 8 * p
        v = blocks[p]
        rows = [jnp.broadcast_to(v[k:k + 1, :], (8, N)) for k in range(8)]
        for m in range(8):
            spread[m, 0:8, :] = jnp.broadcast_to(v[:, base + m:base + m + 1], (8, N))
        s = {(k, m): spread[m, pl.ds(k, 8, stride=0), :] for m in range(8) for k in range(m + 1)}
        columns = {
            (i, k): jnp.broadcast_to(blocks[i][:, base + k:base + k + 1], (8, N))
            for i in range(p + 1, count)
            for k in range(8)
        }
        for cp in stores[4 * p:4 * p + 4]:
            cp.start()
        inverse, u, panel = [], {}, None
        for k in range(8):
            inverse.append(lax.rsqrt(s[k, k]))
            for m in range(k + 1, 8):
                u[k, m] = s[k, m] * inverse[k]
            for m in range(k + 1, 8):
                for q in range(m, 8):
                    s[m, q] = s[m, q] - u[k, m] * u[k, q]
            rows[k] = rows[k] * inverse[k]
            for m in range(k + 1, 8):
                rows[m] = rows[m] - u[k, m] * rows[k]
            panel = rows[k] if panel is None else jnp.where(sub == k, rows[k], panel)
        upper[base:base + 8, :] = jnp.where(lane >= sub + base, panel, 0.0)
        if p == count - 1:
            break
        for k in range(7, -1, -1):
            rows[k] = rows[k] * inverse[k]
            for m in range(k):
                rows[m] = rows[m] - u[m, k] * rows[k]
        for i in range(p + 1, count):
            terms = [columns[i, k] * rows[k] for k in range(8)]
            while len(terms) > 1:
                terms = [terms[t] + terms[t + 1] for t in range(0, len(terms), 2)]
            blocks[i] = blocks[i] - terms[0]
    factor[...] = upper[...].T
    for cp in stores:
        cp.wait()


def per_device(sizes, fields):
    gy, gz, zc = sizes
    yc, xc = gy // CORES, gz // zc
    owners = xc * CORES
    vmem = pl.BlockSpec(memory_space=pltpu.VMEM)
    anywhere = pl.BlockSpec(memory_space=pl.ANY)
    grid_rows = jax.ShapeDtypeStruct((RY, N, RZ), F32)
    dma = pltpu.SemaphoreType.DMA

    def body(*refs):
        main_kernel(sizes, *refs)

    def channel(squares, diags):
        rows = squares * (N // owners) + diags
        return [
            pltpu.VMEM((owners, rows, N), F32),
            pltpu.VMEM((owners - 1, rows, N), F32),
            pltpu.VMEM((rows, N), F32),
            pltpu.VMEM((yc - 1, rows, N), F32),
            pltpu.VMEM((rows, N), F32),
            pltpu.VMEM((zc - 1, rows, N), F32),
            dma((owners - 1,)),
            dma((owners - 1,)),
            dma((yc - 1,)),
            dma((yc - 1,)),
            dma((zc - 1,)),
            dma((zc - 1,)),
        ]

    e, s, cross = pl.pallas_call(
        body,
        out_shape=(grid_rows, grid_rows, jax.ShapeDtypeStruct((N, N), F32)),
        in_specs=[pl.BlockSpec(memory_space=pltpu.HBM)],
        out_specs=(vmem, vmem, vmem),
        scratch_shapes=[
            pltpu.VMEM((3, RY + 4, N + 16, RZ), F32),
            pltpu.VMEM((2, N, RZ), F32),
            pltpu.VMEM((N, RZ), F32),
            pltpu.VMEM((N, RZ), F32),
            pltpu.VMEM((N, RZ), F32),
            pltpu.VMEM((N, RZ), F32),
            pltpu.VMEM((2, N, RZ), F32),
            pltpu.VMEM((3, RY, N, RZ), F32),
            pltpu.VMEM((RY, N, RZ), F32),
            pltpu.VMEM((RY, N, RZ), F32),
            pltpu.VMEM((5, 2 * N, RY * RZ), BF16),
            pltpu.VMEM((2, N, RY * RZ), BF16),
            pltpu.VMEM((2 * RZ, 2 * RZ), BF16),
            pltpu.VMEM((N, N), F32),
            dma((RY,)),
            dma((6,)),
            dma((6,)),
            dma((owners - 1,)),
            dma((owners - 1,)),
            *channel(2, 3),
            *channel(1, 2),
        ],
        compiler_params=pltpu.CompilerParams(collective_id=0, has_side_effects=True, vmem_limit_bytes=48 << 20),
        name="stencil_gram",
    )(pltpu.with_memory_space_constraint(fields, pltpu.HBM))
    whole = jax.ShapeDtypeStruct((N, RY, RZ), F32)
    return pl.pallas_call(
        factor_kernel,
        out_shape=(whole, whole, jax.ShapeDtypeStruct((N, N), F32)),
        in_specs=[vmem, vmem, vmem],
        out_specs=(anywhere, anywhere, vmem),
        scratch_shapes=[
            pltpu.VMEM((N, N), F32),
            pltpu.VMEM((8, 16, N), F32),
            dma((2, RY)),
        ],
        compiler_params=pltpu.CompilerParams(vmem_limit_bytes=16 << 20),
        name="factor",
    )(cross, e, s)


def solution(mesh):
    gy, gz = mesh.shape["gy"], mesh.shape["gz"]
    sizes = (gy, gz, 8 if gz % 8 == 0 else 2)

    def call(fields):
        return per_device(sizes, fields)

    return jax.shard_map(
        call,
        mesh=mesh,
        in_specs=(P(None, None, "gy", "gz"),),
        out_specs=(P(None, "gy", "gz"), P(None, "gy", "gz"), P()),
        check_vma=False,
    )
```
